32 devices in a mesh: depth: 4 (over y, core), tile: 8 (over z, x).
Axes of the slice: x: 2, y: 2, z: 4, core: 2. Of those that a mesh axis runs over, the one named last changes fastest.
Arguments:
- density: float32 [16, 128, 2048], P('depth', 'tile'), may hold values from -6 to 6
- bins: int32 [16, 128, 2048], P('depth', 'tile'), may hold values from 0 to 255
- counts: int32 [4, 8], P('depth', 'tile'), may hold values from 0 to 4
- colors: bfloat16 [3, 256], replicated, may hold values from 0.049804688 to 1
- opacities: bfloat16 [256], replicated, may hold values from 0.0049743652 to 0.19921875
Outputs:
- image: float32 [4, 128, 2048], P(None, 'tile', 'depth')
The draws below stay inside these ranges and needn't reach their ends.
Inputs may be any that keep to these rules, and one draw needn't show every extreme that they name: counts of brick (s, t) is the number of its leading slices that are occupied; its other slices are transparent.
All inputs are finite; a program needn't handle non-finite values.
Results may differ from the reference program's by a relative error of at most 0.0003.
Values sent between devices are 32-bit elements; how exact they have to be, the bound alone decides.
No kernel may reach another device: no remote copies, remote signals or barrier semaphores. Data moves between devices by JAX's collectives and lax.ppermute only.
A program may use at most 64 MiB of HBM per device.

```python
import math
import jax
import jax.numpy as jnp
from jax import lax

DZ = 4
TR = 16
WC = 2048
NBINS = 256
DEPTH = 16
ROWS = 128
N_DEPTH = 4
N_TILE = 8


def place_ends(result, rng, least, largest):
    extent = result.shape
    place = [jax.random.randint(jax.random.fold_in(rng, axis), (), 0, extent[axis]) for axis in range(len(extent))]
    result = result.at[tuple(place)].set(least)
    longest = extent.index(max(extent))
    place[longest] = (place[longest] + 1) % extent[longest]
    return result.at[tuple(place)].set(largest)


def level_of(own_key, shape, cuts, least, largest):
    level = 1.0
    for dim, parts in cuts:
        heights = jax.random.uniform(jax.random.fold_in(jax.random.fold_in(own_key, 6), dim), (parts,), jnp.float32, least / len(cuts), largest / len(cuts))
        level = level * jnp.repeat(jnp.exp(heights), shape[dim] // parts).reshape((-1,) + (1,) * (len(shape) - 1 - dim))
    return level


def scatter_about(stream_key, dims, width, reach, split=(), kind=jnp.bfloat16):
    level = level_of(stream_key, dims, split, -0.22, 0.18) if split else 1.0
    drawn = jax.random.normal(stream_key, dims, jnp.float32) * width * level
    return jnp.minimum(jnp.maximum(drawn, -reach), reach).astype(kind)


def setup_inputs(seed: int = 0) -> dict:
    keys = jax.random.split(jax.random.key(seed), 6)
    return {
        "density": scatter_about(keys[0], (DEPTH, ROWS, WC), 1.0, 6.0, ((0, 4), (1, 8)), jnp.float32),
        "bins": place_ends(jax.random.randint(keys[1], (DEPTH, ROWS, WC), 0, NBINS), jax.random.fold_in(keys[1], 1), 0, NBINS - 1).astype(jnp.int32),
        "counts": place_ends(jax.random.randint(keys[2], (N_DEPTH, N_TILE), 0, DZ + 1), jax.random.fold_in(keys[2], 1), 0, DZ).astype(jnp.int32),
        "colors": jnp.clip(jax.random.uniform(keys[3], (3, NBINS), jnp.float32, 0.049804688, 1.0), 0.049804688, 1.0).astype(jnp.bfloat16),
        "opacities": jnp.clip(jnp.exp(jax.random.uniform(keys[4], (NBINS,), jnp.float32, math.log(0.0049743652), math.log(0.19921875))), 0.0049743652, 0.19921875).astype(jnp.bfloat16),
    }


def lighting(padded):
    grad_depth = (padded[2:, 1:-1] - padded[:-2, 1:-1]) * 0.5
    grad_row = (padded[1:-1, 2:] - padded[1:-1, :-2]) * 0.5
    center = padded[1:-1, 1:-1]
    zero_col = jnp.zeros_like(center[:, :, :1])
    grad_col = (jnp.concatenate([center[:, :, 1:], zero_col], 2) - jnp.concatenate([zero_col, center[:, :, :-1]], 2)) * 0.5
    magnitude = jnp.sqrt(grad_depth * grad_depth + grad_row * grad_row + grad_col * grad_col)
    facing = jnp.abs(0.64 * grad_depth + 0.6 * grad_row + 0.48 * grad_col)
    return 0.3 + 0.7 * facing / jnp.maximum(magnitude, 1.0)

def reference(density, bins, counts, colors, opacities):
    transfer = jnp.concatenate([colors, opacities[None]], 0).astype(jnp.float32)
    slab_of = jnp.arange(DEPTH) // DZ
    local_slice = jnp.arange(DEPTH) % DZ

    def one_tile(tile_id):
        start = tile_id * TR
        tile_block = lax.dynamic_slice_in_dim(density, start, TR, 1)
        above = lax.dynamic_slice_in_dim(density, jnp.maximum(start - 1, 0), 1, 1) * (tile_id > 0).astype(density.dtype)
        below = lax.dynamic_slice_in_dim(density, jnp.minimum(start + TR, ROWS - 1), 1, 1) * (tile_id < N_TILE - 1).astype(density.dtype)
        extended = jnp.concatenate([above, tile_block, below], 1)
        padded = jnp.pad(extended, ((1, 1), (0, 0), (0, 0)))
        shade = lighting(padded)
        tile_bins = lax.dynamic_slice_in_dim(bins, start, TR, 1)
        looked = transfer[:, tile_bins]
        tile_counts = lax.dynamic_index_in_dim(counts, tile_id, 1, keepdims=False)
        occupied = (local_slice < tile_counts[slab_of]).astype(density.dtype)
        alpha = looked[3] * occupied[:, None, None]
        shaded = looked[:3] * shade[None]
        passing = jnp.cumprod(1.0 - alpha, axis=0)
        before = jnp.concatenate([jnp.ones_like(passing[:1]), passing[:-1]], 0)
        weight = before * alpha
        colored = lax.optimization_barrier(jnp.sum(weight[None] * shaded, axis=1))
        return jnp.concatenate([colored, (1.0 - passing[-1])[None]], 0)
    tiles = lax.map(one_tile, jnp.arange(N_TILE))
    return tiles.transpose(1, 0, 2, 3).reshape(4, ROWS, WC)
```

```python
import functools

import jax
import jax.numpy as jnp
from jax import lax
from jax.experimental import pallas as pl
from jax.experimental.pallas import tpu as pltpu
from jax.sharding import PartitionSpec as P

LANES = 128
SUBLANES = 8
COLOR_ONE = 4096.0
OPACITY_ONE = 32768.0
VMEM_LIMIT = 12 * 2**20


def vmem():
    return pl.BlockSpec(memory_space=pltpu.VMEM)


def smem():
    return pl.BlockSpec(memory_space=pltpu.SMEM)


def params():
    return pltpu.CompilerParams(vmem_limit_bytes=VMEM_LIMIT)


def cost(flops, nbytes):
    return pl.CostEstimate(flops=flops, bytes_accessed=nbytes, transcendentals=0)


def f32(*shape):
    return jax.ShapeDtypeStruct(shape, jnp.float32)


def faces_kernel(density, depth_even, depth_odd, row_even, row_odd):
    slices, rows, _ = density.shape
    depth_low = lax.axis_index("depth") & 1 == 0
    tile_low = lax.axis_index("tile") & 1 == 0
    first, last = density[0], density[slices - 1]
    depth_even[...] = jnp.where(depth_low, last, first)
    depth_odd[...] = jnp.where(depth_low, first, last)
    for k in range(slices):
        top, bottom = density[k, 0:1], density[k, rows - 1 : rows]
        row_even[k : k + 1] = jnp.where(tile_low, bottom, top)
        row_odd[k : k + 1] = jnp.where(tile_low, top, bottom)


def trade(x, axis, first):
    count = lax.axis_size(axis)
    pairs = [(i, i + 1) for i in range(first, count - 1, 2)]
    return lax.ppermute(x, axis, pairs + [(b, a) for a, b in pairs])


def whole_number(x, one):
    return (x.astype(jnp.float32) * one).astype(jnp.int32)


def weights_kernel(count, bins, colors, opacities, weighted, passed):
    slices, rows, cols = bins.shape
    color = whole_number(colors[...], COLOR_ONE)
    opacity = whole_number(opacities[...], OPACITY_ONE)
    words = [color[0:1] | (color[1:2] << 16), color[2:3] | (opacity << 16)]
    tables = [
        [jnp.broadcast_to(word[:, i : i + LANES], (SUBLANES, LANES)) for word in words]
        for i in range(0, word_count(colors), LANES)
    ]
    opacity_unit = [
        jnp.where(k < count[0, 0], 1.0 / OPACITY_ONE, 0.0).astype(jnp.float32)
        for k in range(slices)
    ]
    for r in range(0, rows, SUBLANES):
        for c in range(0, cols, LANES):
            at = (slice(r, r + SUBLANES), slice(c, c + LANES))
            before = jnp.full((SUBLANES, LANES), 1.0 / COLOR_ONE, jnp.float32)
            for k in range(slices):
                index = bins[(k, *at)]
                lane = index & (LANES - 1)
                found = [lane_lookup(tables[0][j], lane) for j in range(2)]
                for part in range(1, len(tables)):
                    here = index >= part * LANES
                    found = [
                        jnp.where(here, lane_lookup(tables[part][j], lane), found[j])
                        for j in range(2)
                    ]
                alpha = (found[1] >> 16).astype(jnp.float32) * opacity_unit[k]
                weight = before * alpha
                weighted[(0, k, *at)] = weight * (found[0] & 0xFFFF).astype(jnp.float32)
                weighted[(1, k, *at)] = weight * (found[0] >> 16).astype(jnp.float32)
                weighted[(2, k, *at)] = weight * (found[1] & 0xFFFF).astype(jnp.float32)
                before = before - weight
            passed[at] = before * COLOR_ONE


def word_count(colors):
    return colors.shape[1]


def lane_lookup(table, lane):
    return jnp.take_along_axis(table, lane, axis=1, mode="promise_in_bounds")


def shade_kernel(keeps, density, depth_even, depth_odd, row_even, row_odd, weighted, passed, image):
    slices, rows, cols = density.shape
    half, _, _, piece = image.shape
    me = lax.axis_index("depth")
    mine = me & 1
    depth_is_low = mine == 0
    tile_is_low = lax.axis_index("tile") & 1 == 0
    lane = lax.broadcasted_iota(jnp.int32, (SUBLANES, LANES), 1)
    sub = lax.broadcasted_iota(jnp.int32, (SUBLANES, LANES), 0)
    at_left, at_right = lane == 0, lane == LANES - 1
    at_top, at_bottom = sub == 0, sub == SUBLANES - 1
    groups = rows // SUBLANES

    for i in range(half):
        number = 2 * i + (mine if keeps else 1 - mine)
        for p in range(0, piece, LANES):
            start = pl.multiple_of(number * piece + p, LANES)
            left = pl.multiple_of(jnp.maximum(start - LANES, 0), LANES)
            right = pl.multiple_of(jnp.minimum(start + LANES, cols - LANES), LANES)
            has_left = jnp.where(start > 0, 1.0, 0.0).astype(jnp.float32)
            has_right = jnp.where(start + LANES < cols, 1.0, 0.0).astype(jnp.float32)
            here = pl.ds(start, LANES)
            even_rows, odd_rows = row_even[:, here], row_odd[:, here]
            above_rows = jnp.where(tile_is_low, odd_rows, even_rows)
            below_rows = jnp.where(tile_is_low, even_rows, odd_rows)
            for g in range(groups):
                at = (slice(g * SUBLANES, (g + 1) * SUBLANES), here)
                even_face, odd_face = depth_even[at], depth_odd[at]
                column = [jnp.where(depth_is_low, odd_face, even_face)]
                column += [density[(k, *at)] for k in range(slices)]
                column += [jnp.where(depth_is_low, even_face, odd_face)]
                sums = [jnp.zeros((SUBLANES, LANES), jnp.float32) for _ in range(3)]
                for k in range(slices):
                    v = column[k + 1]
                    band = slice(g * SUBLANES, (g + 1) * SUBLANES)
                    lv = density[k, band, pl.ds(left, LANES)] * has_left
                    rv = density[k, band, pl.ds(right, LANES)] * has_right
                    plus = jnp.where(at_right, pltpu.roll(rv, LANES - 1, 1), pltpu.roll(v, LANES - 1, 1))
                    minus = jnp.where(at_left, pltpu.roll(lv, 1, 1), pltpu.roll(v, 1, 1))
                    by_col = plus - minus
                    if g == 0:
                        edge = jnp.broadcast_to(above_rows[k : k + 1], (SUBLANES, LANES))
                    else:
                        edge = pltpu.roll(density[k, (g - 1) * SUBLANES : g * SUBLANES, here], 1, 0)
                    up = jnp.where(at_top, edge, pltpu.roll(v, 1, 0))
                    if g == groups - 1:
                        edge = jnp.broadcast_to(below_rows[k : k + 1], (SUBLANES, LANES))
                    else:
                        edge = pltpu.roll(density[k, (g + 1) * SUBLANES : (g + 2) * SUBLANES, here], SUBLANES - 1, 0)
                    down = jnp.where(at_bottom, edge, pltpu.roll(v, SUBLANES - 1, 0))
                    by_row = down - up
                    by_depth = column[k + 2] - column[k]
                    square = by_depth * by_depth + by_row * by_row + by_col * by_col
                    facing = jnp.abs(0.448 * by_depth + 0.42 * by_row + 0.336 * by_col)
                    shade = 0.3 + facing * lax.rsqrt(jnp.maximum(square, 4.0))
                    for channel in range(3):
                        sums[channel] = sums[channel] + weighted[(channel, k, *at)] * shade
                out = (slice(g * SUBLANES, (g + 1) * SUBLANES), slice(p, p + LANES))
                for channel in range(3):
                    image[(i, channel, *out)] = sums[channel]
                image[(i, 3, *out)] = 1.0 - passed[at]


def merge_kernel(level, last, kept, received, *outs):
    pieces = kept.shape[0]
    me = lax.axis_index("depth")
    behind = (me >> level) & 1 == 1

    def merged(piece):
        a, b = kept[piece], received[piece]
        front = jnp.where(behind, b, a)
        back = jnp.where(behind, a, b)
        return front + (1.0 - front[3:4]) * back

    if last:
        outs[0][...] = merged(0)
        return
    bit = (me >> (level + 1)) & 1
    for i in range(pieces // 2):
        outs[0][i] = merged(2 * i + bit)
        outs[1][i] = merged(2 * i + 1 - bit)


def on_device(density, bins, counts, colors, opacities):
    slices, rows, cols = density.shape
    slab_count = lax.axis_size("depth")
    half, piece = slab_count // 2, cols // slab_count
    pixels = rows * cols
    faces = pl.pallas_call(
        faces_kernel,
        out_shape=[f32(rows, cols), f32(rows, cols), f32(slices, cols), f32(slices, cols)],
        in_specs=[vmem()],
        out_specs=[vmem()] * 4,
        compiler_params=params(),
        name="faces",
    )(density)
    traded = [
        trade(faces[0], "depth", 0),
        trade(faces[1], "depth", 1),
        trade(faces[2], "tile", 0),
        trade(faces[3], "tile", 1),
    ]
    weighted, passed = pl.pallas_call(
        weights_kernel,
        out_shape=[f32(3, slices, rows, cols), f32(rows, cols)],
        in_specs=[smem(), vmem(), vmem(), vmem()],
        out_specs=[vmem(), vmem()],
        compiler_params=params(),
        cost_estimate=cost(64 * slices * pixels, 16 * slices * pixels),
        name="weights",
    )(counts, bins, colors, opacities[None])

    def shaded(keeps):
        return pl.pallas_call(
            functools.partial(shade_kernel, keeps),
            out_shape=f32(half, 4, rows, piece),
            in_specs=[vmem()] * 7,
            out_specs=vmem(),
            compiler_params=params(),
            cost_estimate=cost(20 * slices * pixels, 8 * slices * pixels),
            name="shade_kept" if keeps else "shade_sent",
        )(density, *traded, weighted, passed)

    outgoing = shaded(False)
    levels = slab_count.bit_length() - 1
    kept = shaded(True)
    for level in range(levels):
        partner = [(i, i ^ 1 << level) for i in range(slab_count)]
        received = lax.ppermute(outgoing, "depth", partner)
        last = level == levels - 1
        left = kept.shape[0] // 2
        shapes = [f32(4, rows, piece)] if last else [f32(left, 4, rows, piece)] * 2
        merged = pl.pallas_call(
            functools.partial(merge_kernel, level, last),
            out_shape=shapes,
            in_specs=[vmem()] * 2,
            out_specs=[vmem()] * len(shapes),
            compiler_params=params(),
            name="merge",
        )(kept, received)
        if last:
            return merged[0]
        kept, outgoing = merged


def solution(mesh):
    return jax.shard_map(
        on_device,
        mesh=mesh,
        in_specs=(P("depth", "tile", None), P("depth", "tile", None), P("depth", "tile"), P(), P()),
        out_specs=P(None, "tile", "depth"),
        check_vma=False,
    )
```

```python
import functools

import jax
import jax.numpy as jnp
from jax import lax
from jax.experimental import pallas as pl
from jax.experimental.pallas import tpu as pltpu
from jax.sharding import PartitionSpec as P

LANES = 128
SUBLANES = 8
COLOR_ONE = 4096.0
OPACITY_ONE = 32768.0
VMEM_LIMIT = 12 * 2**20


def vmem():
    return pl.BlockSpec(memory_space=pltpu.VMEM)


def smem():
    return pl.BlockSpec(memory_space=pltpu.SMEM)


def stay(x):
    return pltpu.with_memory_space_constraint(x, pltpu.HBM)


def params():
    return pltpu.CompilerParams(vmem_limit_bytes=VMEM_LIMIT)


def cost(flops, nbytes):
    return pl.CostEstimate(flops=flops, bytes_accessed=nbytes, transcendentals=0)


def f32(*shape):
    return jax.ShapeDtypeStruct(shape, jnp.float32)


def load_kernel(
    density_in, bins_in, colors_in, opacities_in,
    density, bins, depth_even, depth_odd, row_even, row_odd, tables,
    colors, opacities, done,
):
    moves = [
        (density_in, density),
        (bins_in, bins),
        (colors_in, colors),
        (opacities_in, opacities),
    ]
    copies = [pltpu.make_async_copy(a, b, done.at[i]) for i, (a, b) in enumerate(moves)]
    for copy in copies:
        copy.start()
    slices, rows, _ = density.shape
    depth_low = lax.axis_index("depth") & 1 == 0
    tile_low = lax.axis_index("tile") & 1 == 0
    copies[0].wait()
    first, last = density[0], density[slices - 1]
    depth_even[...] = jnp.where(depth_low, last, first)
    depth_odd[...] = jnp.where(depth_low, first, last)
    for k in range(slices):
        top, bottom = density[k, 0:1], density[k, rows - 1 : rows]
        row_even[k : k + 1] = jnp.where(tile_low, bottom, top)
        row_odd[k : k + 1] = jnp.where(tile_low, top, bottom)
    for copy in copies[1:]:
        copy.wait()
    color = whole_number(colors[...], COLOR_ONE)
    opacity = whole_number(opacities[...].reshape(1, -1), OPACITY_ONE)
    words = [color[0:1] | (color[1:2] << 16), color[2:3] | (opacity << 16)]
    for part in range(tables.shape[0]):
        for j in range(2):
            table = words[j][:, part * LANES : (part + 1) * LANES]
            tables[part, j] = jnp.broadcast_to(table, (SUBLANES, LANES))


def trade(x, axis, first):
    count = lax.axis_size(axis)
    pairs = [(i, (i + 1) % count) for i in range(first, count, 2)]
    return lax.ppermute(x, axis, pairs + [(b, a) for a, b in pairs])


def whole_number(x, one):
    return (x.astype(jnp.float32) * one).astype(jnp.int32)


def weights_kernel(count, bins, tables, weighted, passed):
    slices, rows, cols = bins.shape
    parts = tables.shape[0]
    table = [[tables[part, j] for j in range(2)] for part in range(parts)]
    occupied = count[0, 0]
    unit = [flag(k < occupied) * (1.0 / OPACITY_ONE) for k in range(slices)]
    for r in range(0, rows, SUBLANES):
        for c in range(0, cols, LANES):
            at = (slice(r, r + SUBLANES), slice(c, c + LANES))
            before = jnp.full((SUBLANES, LANES), 1.0 / COLOR_ONE, jnp.float32)
            for k in range(slices):
                index = bins[(k, *at)]
                lane = index & (LANES - 1)
                found = [lane_lookup(table[0][j], lane) for j in range(2)]
                for part in range(1, parts):
                    here = index >= part * LANES
                    found = [
                        jnp.where(here, lane_lookup(table[part][j], lane), found[j])
                        for j in range(2)
                    ]
                alpha = (found[1] >> 16).astype(jnp.float32) * unit[k]
                weight = before * alpha
                weighted[(0, k, *at)] = weight * (found[0] & 0xFFFF).astype(jnp.float32)
                weighted[(1, k, *at)] = weight * (found[0] >> 16).astype(jnp.float32)
                weighted[(2, k, *at)] = weight * (found[1] & 0xFFFF).astype(jnp.float32)
                before = before - weight
            passed[at] = before * COLOR_ONE


def lane_lookup(table, lane):
    return jnp.take_along_axis(table, lane, axis=1, mode="promise_in_bounds")


def flag(condition):
    return jnp.where(condition, 1.0, 0.0).astype(jnp.float32)


def shade_kernel(keeps, density, depth_even, depth_odd, row_even, row_odd, weighted, passed, image):
    slices, rows, cols = density.shape
    half, _, _, piece = image.shape
    me = lax.axis_index("depth")
    mine = me & 1
    depth_is_low = mine == 0
    tile = lax.axis_index("tile")
    tile_is_low = tile & 1 == 0
    has_front, has_behind = flag(me > 0), flag(me < lax.axis_size("depth") - 1)
    has_above, has_below = flag(tile > 0), flag(tile < lax.axis_size("tile") - 1)
    lane = lax.broadcasted_iota(jnp.int32, (SUBLANES, LANES), 1)
    sub = lax.broadcasted_iota(jnp.int32, (SUBLANES, LANES), 0)
    at_left, at_right = lane == 0, lane == LANES - 1
    at_top, at_bottom = sub == 0, sub == SUBLANES - 1
    groups = rows // SUBLANES

    for i in range(half):
        number = 2 * i + (mine if keeps else 1 - mine)
        for p in range(0, piece, LANES):
            start = pl.multiple_of(number * piece + p, LANES)
            left = pl.multiple_of(jnp.maximum(start - LANES, 0), LANES)
            right = pl.multiple_of(jnp.minimum(start + LANES, cols - LANES), LANES)
            has_left = flag(start > 0)
            has_right = flag(start + LANES < cols)
            here = pl.ds(start, LANES)
            even_rows, odd_rows = row_even[:, here], row_odd[:, here]
            above_rows = jnp.where(tile_is_low, odd_rows, even_rows) * has_above
            below_rows = jnp.where(tile_is_low, even_rows, odd_rows) * has_below
            for g in range(groups):
                at = (slice(g * SUBLANES, (g + 1) * SUBLANES), here)
                even_face, odd_face = depth_even[at], depth_odd[at]
                column = [jnp.where(depth_is_low, odd_face, even_face) * has_front]
                column += [density[(k, *at)] for k in range(slices)]
                column += [jnp.where(depth_is_low, even_face, odd_face) * has_behind]
                sums = [jnp.zeros((SUBLANES, LANES), jnp.float32) for _ in range(3)]
                for k in range(slices):
                    v = column[k + 1]
                    band = slice(g * SUBLANES, (g + 1) * SUBLANES)
                    lv = density[k, band, pl.ds(left, LANES)] * has_left
                    rv = density[k, band, pl.ds(right, LANES)] * has_right
                    plus = jnp.where(at_right, pltpu.roll(rv, LANES - 1, 1), pltpu.roll(v, LANES - 1, 1))
                    minus = jnp.where(at_left, pltpu.roll(lv, 1, 1), pltpu.roll(v, 1, 1))
                    by_col = plus - minus
                    if g == 0:
                        edge = jnp.broadcast_to(above_rows[k : k + 1], (SUBLANES, LANES))
                    else:
                        edge = pltpu.roll(density[k, (g - 1) * SUBLANES : g * SUBLANES, here], 1, 0)
                    up = jnp.where(at_top, edge, pltpu.roll(v, 1, 0))
                    if g == groups - 1:
                        edge = jnp.broadcast_to(below_rows[k : k + 1], (SUBLANES, LANES))
                    else:
                        edge = pltpu.roll(density[k, (g + 1) * SUBLANES : (g + 2) * SUBLANES, here], SUBLANES - 1, 0)
                    down = jnp.where(at_bottom, edge, pltpu.roll(v, SUBLANES - 1, 0))
                    by_row = down - up
                    by_depth = column[k + 2] - column[k]
                    square = by_depth * by_depth + by_row * by_row + by_col * by_col
                    facing = jnp.abs(0.448 * by_depth + 0.42 * by_row + 0.336 * by_col)
                    shade = 0.3 + facing * lax.rsqrt(jnp.maximum(square, 4.0))
                    for channel in range(3):
                        sums[channel] = sums[channel] + weighted[(channel, k, *at)] * shade
                out = (slice(g * SUBLANES, (g + 1) * SUBLANES), slice(p, p + LANES))
                for channel in range(3):
                    image[(i, channel, *out)] = sums[channel]
                image[(i, 3, *out)] = 1.0 - passed[at]


def merge_kernel(level, last, kept, received, *outs):
    pieces = kept.shape[0]
    me = lax.axis_index("depth")
    behind = (me >> level) & 1 == 1

    def merged(piece):
        a, b = kept[piece], received[piece]
        front = jnp.where(behind, b, a)
        back = jnp.where(behind, a, b)
        return front + (1.0 - front[3:4]) * back

    if last:
        outs[0][...] = merged(0)
        return
    bit = (me >> (level + 1)) & 1
    for i in range(pieces // 2):
        outs[0][i] = merged(2 * i + bit)
        outs[1][i] = merged(2 * i + 1 - bit)


def on_device(density, bins, counts, colors, opacities):
    slices, rows, cols = density.shape
    slab_count = lax.axis_size("depth")
    half, piece = slab_count // 2, cols // slab_count
    pixels = rows * cols
    parts = opacities.shape[0] // LANES
    here = pl.BlockSpec(memory_space=pltpu.HBM)
    density, bins, *faces, tables = pl.pallas_call(
        load_kernel,
        out_shape=[
            f32(*density.shape),
            jax.ShapeDtypeStruct(bins.shape, jnp.int32),
            f32(rows, cols),
            f32(rows, cols),
            f32(slices, cols),
            f32(slices, cols),
            jax.ShapeDtypeStruct((parts, 2, SUBLANES, LANES), jnp.int32),
        ],
        in_specs=[here] * 4,
        out_specs=[vmem()] * 7,
        scratch_shapes=[
            pltpu.VMEM(colors.shape, colors.dtype),
            pltpu.VMEM(opacities.shape, opacities.dtype),
            pltpu.SemaphoreType.DMA((4,)),
        ],
        compiler_params=params(),
        name="load",
    )(*(stay(x) for x in (density, bins, colors, opacities)))
    traded = [
        trade(faces[0], "depth", 0),
        trade(faces[1], "depth", 1),
        trade(faces[2], "tile", 0),
        trade(faces[3], "tile", 1),
    ]
    weighted, passed = pl.pallas_call(
        weights_kernel,
        out_shape=[f32(3, slices, rows, cols), f32(rows, cols)],
        in_specs=[smem(), vmem(), vmem()],
        out_specs=[vmem(), vmem()],
        compiler_params=params(),
        cost_estimate=cost(64 * slices * pixels, 16 * slices * pixels),
        name="weights",
    )(counts, bins, tables)

    def shaded(keeps):
        return pl.pallas_call(
            functools.partial(shade_kernel, keeps),
            out_shape=f32(half, 4, rows, piece),
            in_specs=[vmem()] * 7,
            out_specs=vmem(),
            compiler_params=params(),
            cost_estimate=cost(20 * slices * pixels, 8 * slices * pixels),
            name="shade_kept" if keeps else "shade_sent",
        )(density, *traded, weighted, passed)

    outgoing = shaded(False)
    levels = slab_count.bit_length() - 1
    kept = shaded(True)
    for level in range(levels):
        partner = [(i, i ^ 1 << level) for i in range(slab_count)]
        received = lax.ppermute(outgoing, "depth", partner)
        last = level == levels - 1
        left = kept.shape[0] // 2
        shapes = [f32(4, rows, piece)] if last else [f32(left, 4, rows, piece)] * 2
        merged = pl.pallas_call(
            functools.partial(merge_kernel, level, last),
            out_shape=shapes,
            in_specs=[vmem()] * 2,
            out_specs=[vmem()] * len(shapes),
            compiler_params=params(),
            name="merge",
        )(kept, received)
        if last:
            return merged[0]
        kept, outgoing = merged


def solution(mesh):
    return jax.shard_map(
        on_device,
        mesh=mesh,
        in_specs=(P("depth", "tile", None), P("depth", "tile", None), P("depth", "tile"), P(), P()),
        out_specs=P(None, "tile", "depth"),
        check_vma=False,
    )
```

```python
import functools

import jax
import jax.numpy as jnp
from jax import lax
from jax.experimental import pallas as pl
from jax.experimental.pallas import tpu as pltpu
from jax.sharding import PartitionSpec as P

LANES = 128
SUBLANES = 8
COLOR_ONE = 4096.0
OPACITY_ONE = 32768.0
VMEM_LIMIT = 12 * 2**20


def vmem():
    return pl.BlockSpec(memory_space=pltpu.VMEM)


def smem():
    return pl.BlockSpec(memory_space=pltpu.SMEM)


def stay(x):
    return pltpu.with_memory_space_constraint(x, pltpu.HBM)


def params():
    return pltpu.CompilerParams(vmem_limit_bytes=VMEM_LIMIT)


def cost(flops, nbytes):
    return pl.CostEstimate(flops=flops, bytes_accessed=nbytes, transcendentals=0)


def f32(*shape):
    return jax.ShapeDtypeStruct(shape, jnp.float32)


def load_kernel(
    density_in, bins_in, colors_in, opacities_in,
    density, bins, depth_even, depth_odd, row_even, row_odd, tables,
    colors, opacities, done,
):
    moves = [
        (density_in, density),
        (bins_in, bins),
        (colors_in, colors),
        (opacities_in, opacities),
    ]
    copies = [pltpu.make_async_copy(a, b, done.at[i]) for i, (a, b) in enumerate(moves)]
    for copy in copies:
        copy.start()
    slices, rows, _ = density.shape
    depth_low = lax.axis_index("depth") & 1 == 0
    tile_low = lax.axis_index("tile") & 1 == 0
    copies[0].wait()
    first, last = density[0], density[slices - 1]
    depth_even[...] = jnp.where(depth_low, last, first)
    depth_odd[...] = jnp.where(depth_low, first, last)
    for k in range(slices):
        top, bottom = density[k, 0:1], density[k, rows - 1 : rows]
        row_even[k : k + 1] = jnp.where(tile_low, bottom, top)
        row_odd[k : k + 1] = jnp.where(tile_low, top, bottom)
    for copy in copies[1:]:
        copy.wait()
    color = whole_number(colors[...], COLOR_ONE)
    opacity = whole_number(opacities[...].reshape(1, -1), OPACITY_ONE)
    words = [color[0:1] | (color[1:2] << 16), color[2:3] | (opacity << 16)]
    for part in range(tables.shape[0]):
        for j in range(2):
            table = words[j][:, part * LANES : (part + 1) * LANES]
            tables[part, j] = jnp.broadcast_to(table, (SUBLANES, LANES))


def trade(x, axis, first):
    slabs, tiles = lax.axis_size("depth"), lax.axis_size("tile")
    pairs = []
    for d in range(slabs):
        for t in range(tiles):
            if axis == "depth":
                inside = 0 <= ((d - first) ^ 1) + first < slabs
                partner = (((d - first) ^ 1) + first, t) if inside else (d, t ^ 1)
            else:
                inside = 0 <= ((t - first) ^ 1) + first < tiles
                partner = (d, ((t - first) ^ 1) + first) if inside else (d ^ 1, t)
            pairs.append((d * tiles + t, partner[0] * tiles + partner[1]))
    return lax.ppermute(x, ("depth", "tile"), pairs)


def whole_number(x, one):
    return (x.astype(jnp.float32) * one).astype(jnp.int32)


def weights_kernel(count, bins, tables, weighted, passed):
    slices, rows, cols = bins.shape
    parts = tables.shape[0]
    table = [[tables[part, j] for j in range(2)] for part in range(parts)]
    occupied = count[0, 0]
    unit = [flag(k < occupied) * (1.0 / OPACITY_ONE) for k in range(slices)]
    for r in range(0, rows, SUBLANES):
        for c in range(0, cols, LANES):
            at = (slice(r, r + SUBLANES), slice(c, c + LANES))
            before = jnp.full((SUBLANES, LANES), 1.0 / COLOR_ONE, jnp.float32)
            for k in range(slices):
                index = bins[(k, *at)]
                lane = index & (LANES - 1)
                found = [lane_lookup(table[0][j], lane) for j in range(2)]
                for part in range(1, parts):
                    here = index >= part * LANES
                    found = [
                        jnp.where(here, lane_lookup(table[part][j], lane), found[j])
                        for j in range(2)
                    ]
                alpha = (found[1] >> 16).astype(jnp.float32) * unit[k]
                weight = before * alpha
                weighted[(0, k, *at)] = weight * (found[0] & 0xFFFF).astype(jnp.float32)
                weighted[(1, k, *at)] = weight * (found[0] >> 16).astype(jnp.float32)
                weighted[(2, k, *at)] = weight * (found[1] & 0xFFFF).astype(jnp.float32)
                before = before - weight
            passed[at] = before * COLOR_ONE


def lane_lookup(table, lane):
    return jnp.take_along_axis(table, lane, axis=1, mode="promise_in_bounds")


def flag(condition):
    return jnp.where(condition, 1.0, 0.0).astype(jnp.float32)


def shade_kernel(keeps, density, depth_even, depth_odd, row_even, row_odd, weighted, passed, image):
    slices, rows, cols = density.shape
    half, _, _, piece = image.shape
    me = lax.axis_index("depth")
    mine = me & 1
    depth_is_low = mine == 0
    tile = lax.axis_index("tile")
    tile_is_low = tile & 1 == 0
    has_front, has_behind = flag(me > 0), flag(me < lax.axis_size("depth") - 1)
    has_above, has_below = flag(tile > 0), flag(tile < lax.axis_size("tile") - 1)
    lane = lax.broadcasted_iota(jnp.int32, (SUBLANES, LANES), 1)
    sub = lax.broadcasted_iota(jnp.int32, (SUBLANES, LANES), 0)
    at_left, at_right = lane == 0, lane == LANES - 1
    at_top, at_bottom = sub == 0, sub == SUBLANES - 1
    groups = rows // SUBLANES

    for i in range(half):
        number = 2 * i + (mine if keeps else 1 - mine)
        for p in range(0, piece, LANES):
            start = pl.multiple_of(number * piece + p, LANES)
            left = pl.multiple_of(jnp.maximum(start - LANES, 0), LANES)
            right = pl.multiple_of(jnp.minimum(start + LANES, cols - LANES), LANES)
            has_left = flag(start > 0)
            has_right = flag(start + LANES < cols)
            here = pl.ds(start, LANES)
            even_rows, odd_rows = row_even[:, here], row_odd[:, here]
            above_rows = jnp.where(tile_is_low, odd_rows, even_rows) * has_above
            below_rows = jnp.where(tile_is_low, even_rows, odd_rows) * has_below
            for g in range(groups):
                at = (slice(g * SUBLANES, (g + 1) * SUBLANES), here)
                even_face, odd_face = depth_even[at], depth_odd[at]
                column = [jnp.where(depth_is_low, odd_face, even_face) * has_front]
                column += [density[(k, *at)] for k in range(slices)]
                column += [jnp.where(depth_is_low, even_face, odd_face) * has_behind]
                sums = [jnp.zeros((SUBLANES, LANES), jnp.float32) for _ in range(3)]
                for k in range(slices):
                    v = column[k + 1]
                    band = slice(g * SUBLANES, (g + 1) * SUBLANES)
                    lv = density[k, band, pl.ds(left, LANES)] * has_left
                    rv = density[k, band, pl.ds(right, LANES)] * has_right
                    plus = jnp.where(at_right, pltpu.roll(rv, LANES - 1, 1), pltpu.roll(v, LANES - 1, 1))
                    minus = jnp.where(at_left, pltpu.roll(lv, 1, 1), pltpu.roll(v, 1, 1))
                    by_col = plus - minus
                    if g == 0:
                        edge = jnp.broadcast_to(above_rows[k : k + 1], (SUBLANES, LANES))
                    else:
                        edge = pltpu.roll(density[k, (g - 1) * SUBLANES : g * SUBLANES, here], 1, 0)
                    up = jnp.where(at_top, edge, pltpu.roll(v, 1, 0))
                    if g == groups - 1:
                        edge = jnp.broadcast_to(below_rows[k : k + 1], (SUBLANES, LANES))
                    else:
                        edge = pltpu.roll(density[k, (g + 1) * SUBLANES : (g + 2) * SUBLANES, here], SUBLANES - 1, 0)
                    down = jnp.where(at_bottom, edge, pltpu.roll(v, SUBLANES - 1, 0))
                    by_row = down - up
                    by_depth = column[k + 2] - column[k]
                    square = by_depth * by_depth + by_row * by_row + by_col * by_col
                    facing = jnp.abs(0.448 * by_depth + 0.42 * by_row + 0.336 * by_col)
                    shade = 0.3 + facing * lax.rsqrt(jnp.maximum(square, 4.0))
                    for channel in range(3):
                        sums[channel] = sums[channel] + weighted[(channel, k, *at)] * shade
                out = (slice(g * SUBLANES, (g + 1) * SUBLANES), slice(p, p + LANES))
                for channel in range(3):
                    image[(i, channel, *out)] = sums[channel]
                image[(i, 3, *out)] = 1.0 - passed[at]


def merge_kernel(level, last, kept, received, *outs):
    pieces = kept.shape[0]
    me = lax.axis_index("depth")
    behind = (me >> level) & 1 == 1

    def merged(piece):
        a, b = kept[piece], received[piece]
        front = jnp.where(behind, b, a)
        back = jnp.where(behind, a, b)
        return front + (1.0 - front[3:4]) * back

    if last:
        outs[0][...] = merged(0)
        return
    bit = (me >> (level + 1)) & 1
    for i in range(pieces // 2):
        outs[0][i] = merged(2 * i + bit)
        outs[1][i] = merged(2 * i + 1 - bit)


def on_device(density, bins, counts, colors, opacities):
    slices, rows, cols = density.shape
    slab_count = lax.axis_size("depth")
    half, piece = slab_count // 2, cols // slab_count
    pixels = rows * cols
    parts = opacities.shape[0] // LANES
    here = pl.BlockSpec(memory_space=pltpu.HBM)
    density, bins, *faces, tables = pl.pallas_call(
        load_kernel,
        out_shape=[
            f32(*density.shape),
            jax.ShapeDtypeStruct(bins.shape, jnp.int32),
            f32(rows, cols),
            f32(rows, cols),
            f32(slices, cols),
            f32(slices, cols),
            jax.ShapeDtypeStruct((parts, 2, SUBLANES, LANES), jnp.int32),
        ],
        in_specs=[here] * 4,
        out_specs=[vmem()] * 7,
        scratch_shapes=[
            pltpu.VMEM(colors.shape, colors.dtype),
            pltpu.VMEM(opacities.shape, opacities.dtype),
            pltpu.SemaphoreType.DMA((4,)),
        ],
        compiler_params=params(),
        name="load",
    )(*(stay(x) for x in (density, bins, colors, opacities)))
    traded = [
        trade(faces[0], "depth", 0),
        trade(faces[1], "depth", 1),
        trade(faces[2], "tile", 0),
        trade(faces[3], "tile", 1),
    ]
    weighted, passed = pl.pallas_call(
        weights_kernel,
        out_shape=[f32(3, slices, rows, cols), f32(rows, cols)],
        in_specs=[smem(), vmem(), vmem()],
        out_specs=[vmem(), vmem()],
        compiler_params=params(),
        cost_estimate=cost(64 * slices * pixels, 16 * slices * pixels),
        name="weights",
    )(counts, bins, tables)

    def shaded(keeps):
        return pl.pallas_call(
            functools.partial(shade_kernel, keeps),
            out_shape=f32(half, 4, rows, piece),
            in_specs=[vmem()] * 7,
            out_specs=vmem(),
            compiler_params=params(),
            cost_estimate=cost(20 * slices * pixels, 8 * slices * pixels),
            name="shade_kept" if keeps else "shade_sent",
        )(density, *traded, weighted, passed)

    outgoing = shaded(False)
    levels = slab_count.bit_length() - 1
    kept = shaded(True)
    for level in range(levels):
        partner = [(i, i ^ 1 << level) for i in range(slab_count)]
        received = lax.ppermute(outgoing, "depth", partner)
        last = level == levels - 1
        left = kept.shape[0] // 2
        shapes = [f32(4, rows, piece)] if last else [f32(left, 4, rows, piece)] * 2
        merged = pl.pallas_call(
            functools.partial(merge_kernel, level, last),
            out_shape=shapes,
            in_specs=[vmem()] * 2,
            out_specs=[vmem()] * len(shapes),
            compiler_params=params(),
            name="merge",
        )(kept, received)
        if last:
            return merged[0]
        kept, outgoing = merged


def solution(mesh):
    return jax.shard_map(
        on_device,
        mesh=mesh,
        in_specs=(P("depth", "tile", None), P("depth", "tile", None), P("depth", "tile"), P(), P()),
        out_specs=P(None, "tile", "depth"),
        check_vma=False,
    )
```

```python
import functools

import jax
import jax.numpy as jnp
from jax import lax
from jax.experimental import pallas as pl
from jax.experimental.pallas import tpu as pltpu
from jax.sharding import PartitionSpec as P

LANES = 128
SUBLANES = 8
COLOR_ONE = 4096.0
OPACITY_ONE = 32768.0
VMEM_LIMIT = 12 * 2**20


def vmem():
    return pl.BlockSpec(memory_space=pltpu.VMEM)


def smem():
    return pl.BlockSpec(memory_space=pltpu.SMEM)


def stay(x):
    return pltpu.with_memory_space_constraint(x, pltpu.HBM)


def params():
    return pltpu.CompilerParams(vmem_limit_bytes=VMEM_LIMIT)


def cost(flops, nbytes):
    return pl.CostEstimate(flops=flops, bytes_accessed=nbytes, transcendentals=0)


def f32(*shape):
    return jax.ShapeDtypeStruct(shape, jnp.float32)


def load_kernel(
    density_in, bins_in, colors_in, opacities_in,
    density, bins, depth_even, depth_odd, row_even, row_odd, tables,
    colors, opacities, done,
):
    moves = [
        (density_in, density),
        (bins_in, bins),
        (colors_in, colors),
        (opacities_in, opacities),
    ]
    copies = [pltpu.make_async_copy(a, b, done.at[i]) for i, (a, b) in enumerate(moves)]
    for copy in copies:
        copy.start()
    slices, rows, _ = density.shape
    depth_low = lax.axis_index("depth") & 1 == 0
    tile_low = lax.axis_index("tile") & 1 == 0
    copies[0].wait()
    first, last = density[0], density[slices - 1]
    depth_even[...] = jnp.where(depth_low, last, first)
    depth_odd[...] = jnp.where(depth_low, first, last)
    for k in range(slices):
        top, bottom = density[k, 0:1], density[k, rows - 1 : rows]
        row_even[k : k + 1] = jnp.where(tile_low, bottom, top)
        row_odd[k : k + 1] = jnp.where(tile_low, top, bottom)
    for copy in copies[1:]:
        copy.wait()
    color = whole_number(colors[...], COLOR_ONE)
    opacity = whole_number(opacities[...].reshape(1, -1), OPACITY_ONE)
    words = [color[0:1] | (color[1:2] << 16), color[2:3] | (opacity << 16)]
    for part in range(tables.shape[0]):
        for j in range(2):
            table = words[j][:, part * LANES : (part + 1) * LANES]
            tables[part, j] = jnp.broadcast_to(table, (SUBLANES, LANES))


def trade(x, axis, first):
    slabs, tiles = lax.axis_size("depth"), lax.axis_size("tile")
    pairs = []
    for d in range(slabs):
        for t in range(tiles):
            if axis == "depth":
                inside = 0 <= ((d - first) ^ 1) + first < slabs
                partner = (((d - first) ^ 1) + first, t) if inside else (d, t ^ 1)
            else:
                inside = 0 <= ((t - first) ^ 1) + first < tiles
                partner = (d, ((t - first) ^ 1) + first) if inside else (d ^ 1, t)
            pairs.append((d * tiles + t, partner[0] * tiles + partner[1]))
    return lax.ppermute(x, ("depth", "tile"), pairs)


def whole_number(x, one):
    return (x.astype(jnp.float32) * one).astype(jnp.int32)


def weights_kernel(count, bins, tables, weighted, passed_kept, passed_sent):
    slices, rows, _ = bins.shape
    half, _, piece = passed_kept.shape
    parts = tables.shape[0]
    table = [[tables[part, j] for j in range(2)] for part in range(parts)]
    occupied = count[0, 0]
    unit = [flag(k < occupied) * (1.0 / OPACITY_ONE) for k in range(slices)]
    mine = lax.axis_index("depth") & 1
    for passed, parity in ((passed_sent, 1 - mine), (passed_kept, mine)):
        for i in range(half):
            for p in range(0, piece, LANES):
                here = pl.ds(pl.multiple_of((2 * i + parity) * piece + p, LANES), LANES)
                for r in range(0, rows, SUBLANES):
                    at = (slice(r, r + SUBLANES), here)
                    before = jnp.full((SUBLANES, LANES), 1.0 / COLOR_ONE, jnp.float32)
                    for k in range(slices):
                        index = bins[(k, *at)]
                        lane = index & (LANES - 1)
                        found = [lane_lookup(table[0][j], lane) for j in range(2)]
                        for part in range(1, parts):
                            later = index >= part * LANES
                            found = [
                                jnp.where(later, lane_lookup(table[part][j], lane), found[j])
                                for j in range(2)
                            ]
                        alpha = (found[1] >> 16).astype(jnp.float32) * unit[k]
                        weight = before * alpha
                        red = (found[0] & 0xFFFF).astype(jnp.float32)
                        green = (found[0] >> 16).astype(jnp.float32)
                        blue = (found[1] & 0xFFFF).astype(jnp.float32)
                        weighted[(0, k, *at)] = weight * red
                        weighted[(1, k, *at)] = weight * green
                        weighted[(2, k, *at)] = weight * blue
                        before = before - weight
                    passed[i, r : r + SUBLANES, p : p + LANES] = before * COLOR_ONE


def lane_lookup(table, lane):
    return jnp.take_along_axis(table, lane, axis=1, mode="promise_in_bounds")


def flag(condition):
    return jnp.where(condition, 1.0, 0.0).astype(jnp.float32)


def shade_kernel(stays, density, depth_even, depth_odd, row_even, row_odd, weighted, image):
    slices, rows, cols = density.shape
    pieces, _, _, piece = image.shape
    me = lax.axis_index("depth")
    mine = me & 1
    bits = [(me >> i) & 1 if stays[i] else 1 - ((me >> i) & 1) for i in range(2)]
    depth_is_low = mine == 0
    tile = lax.axis_index("tile")
    tile_is_low = tile & 1 == 0
    has_front, has_behind = flag(me > 0), flag(me < lax.axis_size("depth") - 1)
    has_above, has_below = flag(tile > 0), flag(tile < lax.axis_size("tile") - 1)
    lane = lax.broadcasted_iota(jnp.int32, (SUBLANES, LANES), 1)
    sub = lax.broadcasted_iota(jnp.int32, (SUBLANES, LANES), 0)
    at_left, at_right = lane == 0, lane == LANES - 1
    at_top, at_bottom = sub == 0, sub == SUBLANES - 1
    groups = rows // SUBLANES

    for i in range(pieces):
        number = 4 * i + 2 * bits[1] + bits[0]
        for p in range(0, piece, LANES):
            start = pl.multiple_of(number * piece + p, LANES)
            left = pl.multiple_of(jnp.maximum(start - LANES, 0), LANES)
            right = pl.multiple_of(jnp.minimum(start + LANES, cols - LANES), LANES)
            has_left = flag(start > 0)
            has_right = flag(start + LANES < cols)
            here = pl.ds(start, LANES)
            even_rows, odd_rows = row_even[:, here], row_odd[:, here]
            above_rows = jnp.where(tile_is_low, odd_rows, even_rows) * has_above
            below_rows = jnp.where(tile_is_low, even_rows, odd_rows) * has_below
            for g in range(groups):
                at = (slice(g * SUBLANES, (g + 1) * SUBLANES), here)
                even_face, odd_face = depth_even[at], depth_odd[at]
                column = [jnp.where(depth_is_low, odd_face, even_face) * has_front]
                column += [density[(k, *at)] for k in range(slices)]
                column += [jnp.where(depth_is_low, even_face, odd_face) * has_behind]
                sums = [jnp.zeros((SUBLANES, LANES), jnp.float32) for _ in range(3)]
                for k in range(slices):
                    v = column[k + 1]
                    band = slice(g * SUBLANES, (g + 1) * SUBLANES)
                    lv = density[k, band, pl.ds(left, LANES)] * has_left
                    rv = density[k, band, pl.ds(right, LANES)] * has_right
                    plus = jnp.where(at_right, pltpu.roll(rv, LANES - 1, 1), pltpu.roll(v, LANES - 1, 1))
                    minus = jnp.where(at_left, pltpu.roll(lv, 1, 1), pltpu.roll(v, 1, 1))
                    by_col = plus - minus
                    if g == 0:
                        edge = jnp.broadcast_to(above_rows[k : k + 1], (SUBLANES, LANES))
                    else:
                        edge = pltpu.roll(density[k, (g - 1) * SUBLANES : g * SUBLANES, here], 1, 0)
                    up = jnp.where(at_top, edge, pltpu.roll(v, 1, 0))
                    if g == groups - 1:
                        edge = jnp.broadcast_to(below_rows[k : k + 1], (SUBLANES, LANES))
                    else:
                        edge = pltpu.roll(density[k, (g + 1) * SUBLANES : (g + 2) * SUBLANES, here], SUBLANES - 1, 0)
                    down = jnp.where(at_bottom, edge, pltpu.roll(v, SUBLANES - 1, 0))
                    by_row = down - up
                    by_depth = column[k + 2] - column[k]
                    square = by_depth * by_depth + by_row * by_row + by_col * by_col
                    facing = jnp.abs(0.448 * by_depth + 0.42 * by_row + 0.336 * by_col)
                    shade = 0.3 + facing * lax.rsqrt(jnp.maximum(square, 4.0))
                    for channel in range(3):
                        sums[channel] = sums[channel] + weighted[(channel, k, *at)] * shade
                out = (slice(g * SUBLANES, (g + 1) * SUBLANES), slice(p, p + LANES))
                for channel in range(3):
                    image[(i, channel, *out)] = sums[channel]


def passed_kernel(level, kept, received, *outs):
    bit = (lax.axis_index("depth") >> (level + 1)) & 1
    for i in range(kept.shape[0] // 2):
        for out, j in zip(outs, (2 * i + bit, 2 * i + 1 - bit)):
            out[i] = kept[j] * received[j]


def first_merge_kernel(stays, kept, received, passed_kept, passed_received, out):
    me = lax.axis_index("depth")
    bit = (me >> 1) & 1
    for i in range(kept.shape[0]):
        j = 2 * i + (bit if stays else 1 - bit)
        out[i] = merged(me & 1 == 1, kept[i], received[i], passed_kept[j], passed_received[j])


def merged(behind, kept, received, passed_kept, passed_received):
    front = jnp.where(behind, received, kept)
    back = jnp.where(behind, kept, received)
    return front + jnp.where(behind, passed_received, passed_kept)[None] * back


def merge_kernel(level, kept, received, passed_kept, passed_received, *outs):
    me = lax.axis_index("depth")
    behind = (me >> level) & 1 == 1
    bit = (me >> (level + 1)) & 1
    for i in range(kept.shape[0] // 2):
        for out, j in zip(outs, (2 * i + bit, 2 * i + 1 - bit)):
            out[i] = merged(behind, kept[j], received[j], passed_kept[j], passed_received[j])


def last_merge_kernel(level, kept, received, passed_kept, passed_received, out):
    behind = (lax.axis_index("depth") >> level) & 1 == 1
    out[0:3] = merged(behind, kept[0], received[0], passed_kept[0], passed_received[0])
    out[3] = 1.0 - passed_kept[0] * passed_received[0]


def call(kernel, name, out_shape, *args):
    return pl.pallas_call(
        kernel,
        out_shape=out_shape,
        in_specs=[vmem()] * len(args),
        out_specs=jax.tree.map(lambda _: vmem(), out_shape),
        compiler_params=params(),
        name=name,
    )(*args)


def on_device(density, bins, counts, colors, opacities):
    slices, rows, cols = density.shape
    slab_count = lax.axis_size("depth")
    half, piece = slab_count // 2, cols // slab_count
    pixels = rows * cols
    parts = opacities.shape[0] // LANES
    here = pl.BlockSpec(memory_space=pltpu.HBM)
    density, bins, *faces, tables = pl.pallas_call(
        load_kernel,
        out_shape=[
            f32(*density.shape),
            jax.ShapeDtypeStruct(bins.shape, jnp.int32),
            f32(rows, cols),
            f32(rows, cols),
            f32(slices, cols),
            f32(slices, cols),
            jax.ShapeDtypeStruct((parts, 2, SUBLANES, LANES), jnp.int32),
        ],
        in_specs=[here] * 4,
        out_specs=[vmem()] * 7,
        scratch_shapes=[
            pltpu.VMEM(colors.shape, colors.dtype),
            pltpu.VMEM(opacities.shape, opacities.dtype),
            pltpu.SemaphoreType.DMA((4,)),
        ],
        compiler_params=params(),
        name="load",
    )(*(stay(x) for x in (density, bins, colors, opacities)))
    traded = [
        trade(faces[0], "depth", 0),
        trade(faces[1], "depth", 1),
        trade(faces[2], "tile", 0),
        trade(faces[3], "tile", 1),
    ]
    weighted, passed_kept, passed_sent = pl.pallas_call(
        weights_kernel,
        out_shape=[f32(3, slices, rows, cols)] + [f32(half, rows, piece)] * 2,
        in_specs=[smem(), vmem(), vmem()],
        out_specs=[vmem()] * 3,
        compiler_params=params(),
        cost_estimate=cost(64 * slices * pixels, 16 * slices * pixels),
        name="weights",
    )(counts, bins, tables)

    def swap(x, level):
        return lax.ppermute(x, "depth", [(i, i ^ 1 << level) for i in range(slab_count)])

    def shaded(*stays):
        return pl.pallas_call(
            functools.partial(shade_kernel, stays),
            out_shape=f32(half // 2, 3, rows, piece),
            in_specs=[vmem()] * 6,
            out_specs=vmem(),
            compiler_params=params(),
            cost_estimate=cost(10 * slices * pixels, 4 * slices * pixels),
            name="shade",
        )(density, *traded, weighted)

    levels = slab_count.bit_length() - 1
    passed = [(passed_kept, swap(passed_sent, 0))]
    for level in range(levels - 1):
        left = f32(passed[level][0].shape[0] // 2, rows, piece)
        kernel = functools.partial(passed_kernel, level)
        kept, sent = call(kernel, "passed", [left, left], *passed[level])
        passed.append((kept, swap(sent, level + 1)))

    def first_merge(stays):
        received = swap(shaded(False, stays), 0)
        kernel = functools.partial(first_merge_kernel, stays)
        return call(
            kernel, "first_merge", f32(half // 2, 3, rows, piece),
            shaded(True, stays), received, *passed[0],
        )

    sent = first_merge(False)
    received = swap(sent, 1)
    kept = first_merge(True)
    for level in range(1, levels - 1):
        left = f32(kept.shape[0] // 2, 3, rows, piece)
        kernel = functools.partial(merge_kernel, level)
        kept, sent = call(kernel, "merge", [left, left], kept, received, *passed[level])
        received = swap(sent, level + 1)
    kernel = functools.partial(last_merge_kernel, levels - 1)
    return call(kernel, "last_merge", f32(4, rows, piece), kept, received, *passed[-1])


def solution(mesh):
    return jax.shard_map(
        on_device,
        mesh=mesh,
        in_specs=(P("depth", "tile", None), P("depth", "tile", None), P("depth", "tile"), P(), P()),
        out_specs=P(None, "tile", "depth"),
        check_vma=False,
    )
```

```python
import functools

import jax
import jax.numpy as jnp
from jax import lax
from jax.experimental import pallas as pl
from jax.experimental.pallas import tpu as pltpu
from jax.sharding import PartitionSpec as P

LANES = 128
SUBLANES = 8
COLOR_ONE = 4096.0
OPACITY_ONE = 32768.0
VMEM_LIMIT = 12 * 2**20


def vmem():
    return pl.BlockSpec(memory_space=pltpu.VMEM)


def smem():
    return pl.BlockSpec(memory_space=pltpu.SMEM)


def stay(x):
    return pltpu.with_memory_space_constraint(x, pltpu.HBM)


def params():
    return pltpu.CompilerParams(vmem_limit_bytes=VMEM_LIMIT)


def cost(flops, nbytes):
    return pl.CostEstimate(flops=flops, bytes_accessed=nbytes, transcendentals=0)


def f32(*shape):
    return jax.ShapeDtypeStruct(shape, jnp.float32)


def load_kernel(
    density_in, bins_in, colors_in, opacities_in,
    density, bins, depth_even, depth_odd, row_even, row_odd, tables,
    colors, opacities, done,
):
    slices, rows, _ = density.shape
    moves = [(density_in.at[k], density.at[k]) for k in range(slices)]
    moves += [(bins_in.at[k], bins.at[k]) for k in range(slices)]
    moves += [(colors_in, colors), (opacities_in, opacities)]
    copies = [pltpu.make_async_copy(a, b, done.at[i]) for i, (a, b) in enumerate(moves)]
    for copy in copies:
        copy.start()
    depth_low = lax.axis_index("depth") & 1 == 0
    tile_low = lax.axis_index("tile") & 1 == 0
    for copy in copies[:slices]:
        copy.wait()
    first, last = density[0], density[slices - 1]
    depth_even[...] = jnp.where(depth_low, last, first)
    depth_odd[...] = jnp.where(depth_low, first, last)
    for k in range(slices):
        top, bottom = density[k, 0:1], density[k, rows - 1 : rows]
        row_even[k : k + 1] = jnp.where(tile_low, bottom, top)
        row_odd[k : k + 1] = jnp.where(tile_low, top, bottom)
    for copy in copies[slices:]:
        copy.wait()
    color = whole_number(colors[...], COLOR_ONE)
    opacity = whole_number(opacities[...].reshape(1, -1), OPACITY_ONE)
    words = [color[0:1] | (color[1:2] << 16), color[2:3] | (opacity << 16)]
    for part in range(tables.shape[0]):
        for j in range(2):
            table = words[j][:, part * LANES : (part + 1) * LANES]
            tables[part, j] = jnp.broadcast_to(table, (SUBLANES, LANES))


def trade(x, axis, first):
    slabs, tiles = lax.axis_size("depth"), lax.axis_size("tile")
    pairs = []
    for d in range(slabs):
        for t in range(tiles):
            if axis == "depth":
                inside = 0 <= ((d - first) ^ 1) + first < slabs
                partner = (((d - first) ^ 1) + first, t) if inside else (d, t ^ 1)
            else:
                inside = 0 <= ((t - first) ^ 1) + first < tiles
                partner = (d, ((t - first) ^ 1) + first) if inside else (d ^ 1, t)
            pairs.append((d * tiles + t, partner[0] * tiles + partner[1]))
    return lax.ppermute(x, ("depth", "tile"), pairs)


def whole_number(x, one):
    return (x.astype(jnp.float32) * one).astype(jnp.int32)


def weights_kernel(count, bins, tables, weighted, passed):
    slices, rows, cols = bins.shape
    parts = tables.shape[0]
    table = [[tables[part, j] for j in range(2)] for part in range(parts)]
    occupied = count[0, 0]
    unit = [flag(k < occupied) * (1.0 / OPACITY_ONE) for k in range(slices)]
    for r in range(0, rows, SUBLANES):
        for c in range(0, cols, LANES):
            at = (slice(r, r + SUBLANES), slice(c, c + LANES))
            before = jnp.full((SUBLANES, LANES), 1.0 / COLOR_ONE, jnp.float32)
            for k in range(slices):
                index = bins[(k, *at)]
                lane = index & (LANES - 1)
                found = [lane_lookup(table[0][j], lane) for j in range(2)]
                for part in range(1, parts):
                    later = index >= part * LANES
                    found = [
                        jnp.where(later, lane_lookup(table[part][j], lane), found[j])
                        for j in range(2)
                    ]
                alpha = (found[1] >> 16).astype(jnp.float32) * unit[k]
                weight = before * alpha
                weighted[(0, k, *at)] = weight * (found[0] & 0xFFFF).astype(jnp.float32)
                weighted[(1, k, *at)] = weight * (found[0] >> 16).astype(jnp.float32)
                weighted[(2, k, *at)] = weight * (found[1] & 0xFFFF).astype(jnp.float32)
                before = before - weight
            passed[at] = before * COLOR_ONE


def lane_lookup(table, lane):
    return jnp.take_along_axis(table, lane, axis=1, mode="promise_in_bounds")


def flag(condition):
    return jnp.where(condition, 1.0, 0.0).astype(jnp.float32)


def shade_kernel(stays, top, density, depth_even, depth_odd, row_even, row_odd, weighted, passed, image):
    slices, rows, cols = density.shape
    pieces, _, image_rows, piece = image.shape
    me = lax.axis_index("depth")
    mine = me & 1
    bits = [(me >> i) & 1 if stays[i] else 1 - ((me >> i) & 1) for i in range(2)]
    depth_is_low = mine == 0
    tile = lax.axis_index("tile")
    tile_is_low = tile & 1 == 0
    has_front, has_behind = flag(me > 0), flag(me < lax.axis_size("depth") - 1)
    has_above, has_below = flag(tile > 0), flag(tile < lax.axis_size("tile") - 1)
    lane = lax.broadcasted_iota(jnp.int32, (SUBLANES, LANES), 1)
    sub = lax.broadcasted_iota(jnp.int32, (SUBLANES, LANES), 0)
    at_left, at_right = lane == 0, lane == LANES - 1
    at_top, at_bottom = sub == 0, sub == SUBLANES - 1
    groups = rows // SUBLANES

    for i in range(pieces):
        number = 4 * i + 2 * bits[1] + bits[0]
        for p in range(0, piece, LANES):
            start = pl.multiple_of(number * piece + p, LANES)
            left = pl.multiple_of(jnp.maximum(start - LANES, 0), LANES)
            right = pl.multiple_of(jnp.minimum(start + LANES, cols - LANES), LANES)
            has_left = flag(start > 0)
            has_right = flag(start + LANES < cols)
            here = pl.ds(start, LANES)
            even_rows, odd_rows = row_even[:, here], row_odd[:, here]
            above_rows = jnp.where(tile_is_low, odd_rows, even_rows) * has_above
            below_rows = jnp.where(tile_is_low, even_rows, odd_rows) * has_below
            for g in range(top // SUBLANES, (top + image_rows) // SUBLANES):
                at = (slice(g * SUBLANES, (g + 1) * SUBLANES), here)
                even_face, odd_face = depth_even[at], depth_odd[at]
                column = [jnp.where(depth_is_low, odd_face, even_face) * has_front]
                column += [density[(k, *at)] for k in range(slices)]
                column += [jnp.where(depth_is_low, even_face, odd_face) * has_behind]
                sums = [jnp.zeros((SUBLANES, LANES), jnp.float32) for _ in range(3)]
                for k in range(slices):
                    v = column[k + 1]
                    band = slice(g * SUBLANES, (g + 1) * SUBLANES)
                    lv = density[k, band, pl.ds(left, LANES)] * has_left
                    rv = density[k, band, pl.ds(right, LANES)] * has_right
                    plus = jnp.where(at_right, pltpu.roll(rv, LANES - 1, 1), pltpu.roll(v, LANES - 1, 1))
                    minus = jnp.where(at_left, pltpu.roll(lv, 1, 1), pltpu.roll(v, 1, 1))
                    by_col = plus - minus
                    if g == 0:
                        edge = jnp.broadcast_to(above_rows[k : k + 1], (SUBLANES, LANES))
                    else:
                        edge = pltpu.roll(density[k, (g - 1) * SUBLANES : g * SUBLANES, here], 1, 0)
                    up = jnp.where(at_top, edge, pltpu.roll(v, 1, 0))
                    if g == groups - 1:
                        edge = jnp.broadcast_to(below_rows[k : k + 1], (SUBLANES, LANES))
                    else:
                        edge = pltpu.roll(density[k, (g + 1) * SUBLANES : (g + 2) * SUBLANES, here], SUBLANES - 1, 0)
                    down = jnp.where(at_bottom, edge, pltpu.roll(v, SUBLANES - 1, 0))
                    by_row = down - up
                    by_depth = column[k + 2] - column[k]
                    square = by_depth * by_depth + by_row * by_row + by_col * by_col
                    facing = jnp.abs(0.448 * by_depth + 0.42 * by_row + 0.336 * by_col)
                    shade = 0.3 + facing * lax.rsqrt(jnp.maximum(square, 4.0))
                    for channel in range(3):
                        sums[channel] = sums[channel] + weighted[(channel, k, *at)] * shade
                r = g * SUBLANES - top
                out = (slice(r, r + SUBLANES), slice(p, p + LANES))
                for channel in range(3):
                    image[(i, channel, *out)] = sums[channel]
                image[(i, 3, *out)] = passed[at]


def merged(behind, kept, received):
    front = jnp.where(behind, received, kept)
    back = jnp.where(behind, kept, received)
    light = front[0:3] + front[3:4] * back[0:3]
    return light, front[3] * back[3]


def first_merge_kernel(kept, received, out):
    behind = lax.axis_index("depth") & 1 == 1
    for i in range(kept.shape[0]):
        out[i, 0:3], out[i, 3] = merged(behind, kept[i], received[i])


def merge_kernel(level, bands, kept, *rest):
    me = lax.axis_index("depth")
    behind = (me >> level) & 1 == 1
    bit = (me >> (level + 1)) & 1
    received, (kept_out, *sent) = rest[:bands], rest[bands:]
    height = kept.shape[2] // bands
    for i in range(kept.shape[0] // 2):
        for band in range(bands):
            rows = slice(band * height, (band + 1) * height)
            j = 2 * i + bit
            light, through = merged(behind, kept[j, :, rows], received[band][j])
            kept_out[i, 0:3, rows], kept_out[i, 3, rows] = light, through
            j = 2 * i + 1 - bit
            light, through = merged(behind, kept[j, :, rows], received[band][j])
            sent[band][i, 0:3], sent[band][i, 3] = light, through


def last_merge_kernel(level, bands, kept, *rest):
    behind = (lax.axis_index("depth") >> level) & 1 == 1
    received, out = rest[:bands], rest[bands]
    height = kept.shape[2] // bands
    for band in range(bands):
        rows = slice(band * height, (band + 1) * height)
        light, through = merged(behind, kept[0, :, rows], received[band][0])
        out[0:3, rows], out[3, rows] = light, 1.0 - through


def call(kernel, name, out_shape, *args):
    return pl.pallas_call(
        kernel,
        out_shape=out_shape,
        in_specs=[vmem()] * len(args),
        out_specs=jax.tree.map(lambda _: vmem(), out_shape),
        compiler_params=params(),
        name=name,
    )(*args)


def on_device(density, bins, counts, colors, opacities):
    slices, rows, cols = density.shape
    slab_count = lax.axis_size("depth")
    half, piece = slab_count // 2, cols // slab_count
    pixels = rows * cols
    parts = opacities.shape[0] // LANES
    here = pl.BlockSpec(memory_space=pltpu.HBM)
    density, bins, *faces, tables = pl.pallas_call(
        load_kernel,
        out_shape=[
            f32(*density.shape),
            jax.ShapeDtypeStruct(bins.shape, jnp.int32),
            f32(rows, cols),
            f32(rows, cols),
            f32(slices, cols),
            f32(slices, cols),
            jax.ShapeDtypeStruct((parts, 2, SUBLANES, LANES), jnp.int32),
        ],
        in_specs=[here] * 4,
        out_specs=[vmem()] * 7,
        scratch_shapes=[
            pltpu.VMEM(colors.shape, colors.dtype),
            pltpu.VMEM(opacities.shape, opacities.dtype),
            pltpu.SemaphoreType.DMA((2 * slices + 2,)),
        ],
        compiler_params=params(),
        name="load",
    )(*(stay(x) for x in (density, bins, colors, opacities)))
    traded = [
        trade(faces[0], "depth", 0),
        trade(faces[1], "depth", 1),
        trade(faces[2], "tile", 0),
        trade(faces[3], "tile", 1),
    ]
    weighted, passed = pl.pallas_call(
        weights_kernel,
        out_shape=[f32(3, slices, rows, cols), f32(rows, cols)],
        in_specs=[smem(), vmem(), vmem()],
        out_specs=[vmem()] * 2,
        compiler_params=params(),
        cost_estimate=cost(64 * slices * pixels, 16 * slices * pixels),
        name="weights",
    )(counts, bins, tables)

    def swap(x, level):
        return lax.ppermute(x, "depth", [(i, i ^ 1 << level) for i in range(slab_count)])

    def shaded(stays, top, height):
        return pl.pallas_call(
            functools.partial(shade_kernel, stays, top),
            out_shape=f32(half // 2, 4, height, piece),
            in_specs=[vmem()] * 7,
            out_specs=vmem(),
            compiler_params=params(),
            cost_estimate=cost(5 * slices * pixels, 2 * slices * pixels),
            name="shade",
        )(density, *traded, weighted, passed)

    def first_merge(stays, top, height):
        received = swap(shaded((False, stays), top, height), 0)
        kept = shaded((True, stays), top, height)
        return call(first_merge_kernel, "first_merge", f32(half // 2, 4, height, piece), kept, received)

    levels = slab_count.bit_length() - 1
    bands = rows // SUBLANES
    received = [swap(first_merge(False, band * SUBLANES, SUBLANES), 1) for band in range(bands)]
    kept = first_merge(True, 0, rows)
    for level in range(1, levels - 1):
        left = kept.shape[0] // 2
        shapes = [f32(left, 4, rows, piece)] + [f32(left, 4, SUBLANES, piece)] * bands
        kernel = functools.partial(merge_kernel, level, bands)
        kept, *sent = call(kernel, "merge", shapes, kept, *received)
        received = [swap(x, level + 1) for x in sent]
    kernel = functools.partial(last_merge_kernel, levels - 1, bands)
    return call(kernel, "last_merge", f32(4, rows, piece), kept, *received)


def solution(mesh):
    return jax.shard_map(
        on_device,
        mesh=mesh,
        in_specs=(P("depth", "tile", None), P("depth", "tile", None), P("depth", "tile"), P(), P()),
        out_specs=P(None, "tile", "depth"),
        check_vma=False,
    )
```

```python
import functools

import jax
import jax.numpy as jnp
from jax import lax
from jax.experimental import pallas as pl
from jax.experimental.pallas import tpu as pltpu
from jax.sharding import PartitionSpec as P

LANES = 128
SUBLANES = 8
COLOR_ONE = 4096.0
OPACITY_ONE = 32768.0
VMEM_LIMIT = 12 * 2**20


def vmem():
    return pl.BlockSpec(memory_space=pltpu.VMEM)


def smem():
    return pl.BlockSpec(memory_space=pltpu.SMEM)


def stay(x):
    return pltpu.with_memory_space_constraint(x, pltpu.HBM)


def params():
    return pltpu.CompilerParams(vmem_limit_bytes=VMEM_LIMIT)


def cost(flops, nbytes):
    return pl.CostEstimate(flops=flops, bytes_accessed=nbytes, transcendentals=0)


def f32(*shape):
    return jax.ShapeDtypeStruct(shape, jnp.float32)


def load_kernel(
    density_in, bins_in, colors_in, opacities_in,
    density, bins, depth_even, depth_odd, row_even, row_odd, tables,
    colors, opacities, done,
):
    slices, rows, _ = density.shape
    moves = [
        (density_in, density),
        (bins_in, bins),
        (colors_in, colors),
        (opacities_in, opacities),
    ]
    copies = [pltpu.make_async_copy(a, b, done.at[i]) for i, (a, b) in enumerate(moves)]
    for copy in copies:
        copy.start()
    depth_low = lax.axis_index("depth") & 1 == 0
    tile_low = lax.axis_index("tile") & 1 == 0
    copies[0].wait()
    first, last = density[0], density[slices - 1]
    depth_even[...] = jnp.where(depth_low, last, first)
    depth_odd[...] = jnp.where(depth_low, first, last)
    for k in range(slices):
        top, bottom = density[k, 0:1], density[k, rows - 1 : rows]
        row_even[k : k + 1] = jnp.where(tile_low, bottom, top)
        row_odd[k : k + 1] = jnp.where(tile_low, top, bottom)
    for copy in copies[1:]:
        copy.wait()
    color = whole_number(colors[...], COLOR_ONE)
    opacity = whole_number(opacities[...].reshape(1, -1), OPACITY_ONE)
    words = [color[0:1] | (color[1:2] << 16), color[2:3] | (opacity << 16)]
    for part in range(tables.shape[0]):
        for j in range(2):
            table = words[j][:, part * LANES : (part + 1) * LANES]
            tables[part, j] = jnp.broadcast_to(table, (SUBLANES, LANES))


def trade(x, axis, first):
    slabs, tiles = lax.axis_size("depth"), lax.axis_size("tile")
    pairs = []
    for d in range(slabs):
        for t in range(tiles):
            if axis == "depth":
                inside = 0 <= ((d - first) ^ 1) + first < slabs
                partner = (((d - first) ^ 1) + first, t) if inside else (d, t ^ 1)
            else:
                inside = 0 <= ((t - first) ^ 1) + first < tiles
                partner = (d, ((t - first) ^ 1) + first) if inside else (d ^ 1, t)
            pairs.append((d * tiles + t, partner[0] * tiles + partner[1]))
    return lax.ppermute(x, ("depth", "tile"), pairs)


def whole_number(x, one):
    return (x.astype(jnp.float32) * one).astype(jnp.int32)


def weights_kernel(count, bins, tables, weighted, passed):
    slices, rows, cols = bins.shape
    parts = tables.shape[0]
    table = [[tables[part, j] for j in range(2)] for part in range(parts)]
    occupied = count[0, 0]
    unit = [flag(k < occupied) * (1.0 / OPACITY_ONE) for k in range(slices)]
    for r in range(0, rows, SUBLANES):
        for c in range(0, cols, LANES):
            at = (slice(r, r + SUBLANES), slice(c, c + LANES))
            before = jnp.full((SUBLANES, LANES), 1.0 / COLOR_ONE, jnp.float32)
            for k in range(slices):
                index = bins[(k, *at)]
                lane = index & (LANES - 1)
                found = [lane_lookup(table[0][j], lane) for j in range(2)]
                for part in range(1, parts):
                    later = index >= part * LANES
                    found = [
                        jnp.where(later, lane_lookup(table[part][j], lane), found[j])
                        for j in range(2)
                    ]
                alpha = (found[1] >> 16).astype(jnp.float32) * unit[k]
                weight = before * alpha
                weighted[(0, k, *at)] = weight * (found[0] & 0xFFFF).astype(jnp.float32)
                weighted[(1, k, *at)] = weight * (found[0] >> 16).astype(jnp.float32)
                weighted[(2, k, *at)] = weight * (found[1] & 0xFFFF).astype(jnp.float32)
                before = before - weight
            passed[at] = before * COLOR_ONE


def lane_lookup(table, lane):
    return jnp.take_along_axis(table, lane, axis=1, mode="promise_in_bounds")


def flag(condition):
    return jnp.where(condition, 1.0, 0.0).astype(jnp.float32)


EVEN, ODD = 0, 1


def lower(band):
    tile_is_low = 1 - (lax.axis_index("tile") & 1)
    return tile_is_low if band == EVEN else 1 - tile_is_low


def shade_kernel(stays, bands, density, depth_even, depth_odd, weighted, passed, *rest):
    trades, image = rest[:-1], rest[-1]
    slices, rows, cols = density.shape
    pieces, _, _, piece = image.shape
    me, tile = lax.axis_index("depth"), lax.axis_index("tile")
    bits = [(me >> i) & 1 if stays[i] else 1 - ((me >> i) & 1) for i in range(2)]
    depth_is_low = me & 1 == 0
    has_front, has_behind = flag(me > 0), flag(me < lax.axis_size("depth") - 1)
    inside = flag(jnp.logical_and(tile > 0, tile < lax.axis_size("tile") - 1))
    lane = lax.broadcasted_iota(jnp.int32, (SUBLANES, LANES), 1)
    sub = lax.broadcasted_iota(jnp.int32, (SUBLANES, LANES), 0)
    at_left, at_right = lane == 0, lane == LANES - 1
    at_top, at_bottom = sub == 0, sub == SUBLANES - 1

    for i in range(pieces):
        number = 4 * i + 2 * bits[1] + bits[0]
        for p in range(0, piece, LANES):
            start = pl.multiple_of(number * piece + p, LANES)
            left = pl.multiple_of(jnp.maximum(start - LANES, 0), LANES)
            right = pl.multiple_of(jnp.minimum(start + LANES, cols - LANES), LANES)
            has_left, has_right = flag(start > 0), flag(start + LANES < cols)
            here = pl.ds(start, LANES)
            for n, (band, traded) in enumerate(zip(bands, trades)):
                is_lower = lower(band)
                band_rows = pl.ds(pl.multiple_of(is_lower * SUBLANES, SUBLANES), SUBLANES)
                other_rows = pl.ds(pl.multiple_of((1 - is_lower) * SUBLANES, SUBLANES), SUBLANES)
                is_lower = is_lower == 1
                at = (band_rows, here)
                even_face, odd_face = depth_even[at], depth_odd[at]
                column = [jnp.where(depth_is_low, odd_face, even_face) * has_front]
                column += [density[(k, *at)] for k in range(slices)]
                column += [jnp.where(depth_is_low, even_face, odd_face) * has_behind]
                outside = traded[:, here]
                if band == ODD:
                    outside = outside * inside
                sums = [jnp.zeros((SUBLANES, LANES), jnp.float32) for _ in range(3)]
                for k in range(slices):
                    v = column[k + 1]
                    lv = density[k, band_rows, pl.ds(left, LANES)] * has_left
                    rv = density[k, band_rows, pl.ds(right, LANES)] * has_right
                    plus = jnp.where(at_right, pltpu.roll(rv, LANES - 1, 1), pltpu.roll(v, LANES - 1, 1))
                    minus = jnp.where(at_left, pltpu.roll(lv, 1, 1), pltpu.roll(v, 1, 1))
                    by_col = plus - minus
                    far = jnp.broadcast_to(outside[k : k + 1], (SUBLANES, LANES))
                    other = density[k, other_rows, here]
                    above = jnp.where(is_lower, pltpu.roll(other, 1, 0), far)
                    below = jnp.where(is_lower, far, pltpu.roll(other, SUBLANES - 1, 0))
                    up = jnp.where(at_top, above, pltpu.roll(v, 1, 0))
                    down = jnp.where(at_bottom, below, pltpu.roll(v, SUBLANES - 1, 0))
                    by_row = down - up
                    by_depth = column[k + 2] - column[k]
                    square = by_depth * by_depth + by_row * by_row + by_col * by_col
                    facing = jnp.abs(0.448 * by_depth + 0.42 * by_row + 0.336 * by_col)
                    shade = 0.3 + facing * lax.rsqrt(jnp.maximum(square, 4.0))
                    for channel in range(3):
                        sums[channel] = sums[channel] + weighted[(channel, k, *at)] * shade
                out = (slice(n * SUBLANES, (n + 1) * SUBLANES), slice(p, p + LANES))
                for channel in range(3):
                    image[(i, channel, *out)] = sums[channel]
                image[(i, 3, *out)] = passed[at]


def merged(behind, kept, received):
    front = jnp.where(behind, received, kept)
    back = jnp.where(behind, kept, received)
    light = front[0:3] + front[3:4] * back[0:3]
    return light, front[3] * back[3]


def first_merge_kernel(kept, received, out):
    behind = lax.axis_index("depth") & 1 == 1
    for i in range(kept.shape[0]):
        out[i, 0:3], out[i, 3] = merged(behind, kept[i], received[i])


def merge_kernel(level, bands, kept, *rest):
    me = lax.axis_index("depth")
    behind = (me >> level) & 1 == 1
    bit = (me >> (level + 1)) & 1
    received, (kept_out, *sent) = rest[:bands], rest[bands:]
    height = kept.shape[2] // bands
    for i in range(kept.shape[0] // 2):
        for band in range(bands):
            rows = slice(band * height, (band + 1) * height)
            j = 2 * i + bit
            light, through = merged(behind, kept[j, :, rows], received[band][j])
            kept_out[i, 0:3, rows], kept_out[i, 3, rows] = light, through
            j = 2 * i + 1 - bit
            light, through = merged(behind, kept[j, :, rows], received[band][j])
            sent[band][i, 0:3], sent[band][i, 3] = light, through


def last_merge_kernel(level, bands, kept, *rest):
    behind = (lax.axis_index("depth") >> level) & 1 == 1
    received, out = rest[:bands], rest[bands]
    height = kept.shape[2] // bands
    for band in range(bands):
        rows = slice(band * height, (band + 1) * height)
        light, through = merged(behind, kept[0, :, rows], received[band][0])
        place = pl.ds(pl.multiple_of(lower(band) * SUBLANES, SUBLANES), SUBLANES)
        out[0:3, place], out[3, place] = light, 1.0 - through


def call(kernel, name, out_shape, *args):
    return pl.pallas_call(
        kernel,
        out_shape=out_shape,
        in_specs=[vmem()] * len(args),
        out_specs=jax.tree.map(lambda _: vmem(), out_shape),
        compiler_params=params(),
        name=name,
    )(*args)


def on_device(density, bins, counts, colors, opacities):
    slices, rows, cols = density.shape
    slab_count = lax.axis_size("depth")
    half, piece = slab_count // 2, cols // slab_count
    pixels = rows * cols
    parts = opacities.shape[0] // LANES
    here = pl.BlockSpec(memory_space=pltpu.HBM)
    density, bins, *faces, tables = pl.pallas_call(
        load_kernel,
        out_shape=[
            f32(*density.shape),
            jax.ShapeDtypeStruct(bins.shape, jnp.int32),
            f32(rows, cols),
            f32(rows, cols),
            f32(slices, cols),
            f32(slices, cols),
            jax.ShapeDtypeStruct((parts, 2, SUBLANES, LANES), jnp.int32),
        ],
        in_specs=[here] * 4,
        out_specs=[vmem()] * 7,
        scratch_shapes=[
            pltpu.VMEM(colors.shape, colors.dtype),
            pltpu.VMEM(opacities.shape, opacities.dtype),
            pltpu.SemaphoreType.DMA((4,)),
        ],
        compiler_params=params(),
        name="load",
    )(*(stay(x) for x in (density, bins, colors, opacities)))
    traded = [
        trade(faces[0], "depth", 0),
        trade(faces[1], "depth", 1),
        trade(faces[2], "tile", 0),
        trade(faces[3], "tile", 1),
    ]
    weighted, passed = pl.pallas_call(
        weights_kernel,
        out_shape=[f32(3, slices, rows, cols), f32(rows, cols)],
        in_specs=[smem(), vmem(), vmem()],
        out_specs=[vmem()] * 2,
        compiler_params=params(),
        cost_estimate=cost(64 * slices * pixels, 16 * slices * pixels),
        name="weights",
    )(counts, bins, tables)

    def swap(x, level):
        return lax.ppermute(x, "depth", [(i, i ^ 1 << level) for i in range(slab_count)])

    *faces, row_even, row_odd = traded
    rows_of = {EVEN: row_even, ODD: row_odd}

    def shaded(stays, bands):
        return pl.pallas_call(
            functools.partial(shade_kernel, stays, bands),
            out_shape=f32(half // 2, 4, SUBLANES * len(bands), piece),
            in_specs=[vmem()] * (5 + len(bands)),
            out_specs=vmem(),
            compiler_params=params(),
            cost_estimate=cost(5 * slices * pixels, 2 * slices * pixels),
            name="shade",
        )(density, *faces, weighted, passed, *(rows_of[band] for band in bands))

    levels = slab_count.bit_length() - 1
    bands = (EVEN, ODD)
    sent_far = []
    for band in bands:
        sent = shaded((False, False), (band,))
        received = swap(sent, 0)
        kept = shaded((True, False), (band,))
        _, kept, weighted = lax.optimization_barrier((sent, kept, weighted))
        if sent_far:
            _, kept = lax.optimization_barrier((sent_far[-1], kept))
        sent_far.append(call(first_merge_kernel, "first_merge", f32(*kept.shape), kept, received))
    received = [swap(x, 1) for x in sent_far]
    sent, kept = shaded((False, True), bands), shaded((True, True), bands)
    kept = call(first_merge_kernel, "first_merge", f32(*kept.shape), kept, swap(sent, 0))
    for level in range(1, levels - 1):
        left = kept.shape[0] // 2
        shapes = [f32(left, 4, rows, piece)] + [f32(left, 4, SUBLANES, piece)] * len(bands)
        kernel = functools.partial(merge_kernel, level, len(bands))
        kept, *sent = call(kernel, "merge", shapes, kept, *received)
        received = [swap(x, level + 1) for x in sent]
    kernel = functools.partial(last_merge_kernel, levels - 1, len(bands))
    return call(kernel, "last_merge", f32(4, rows, piece), kept, *received)


def solution(mesh):
    return jax.shard_map(
        on_device,
        mesh=mesh,
        in_specs=(P("depth", "tile", None), P("depth", "tile", None), P("depth", "tile"), P(), P()),
        out_specs=P(None, "tile", "depth"),
        check_vma=False,
    )
```

```python
import functools

import jax
import jax.numpy as jnp
from jax import lax
from jax.experimental import pallas as pl
from jax.experimental.pallas import tpu as pltpu
from jax.sharding import PartitionSpec as P

LANES = 128
SUBLANES = 8
COLOR_ONE = 4096.0
OPACITY_ONE = 32768.0
VMEM_LIMIT = 12 * 2**20


def vmem():
    return pl.BlockSpec(memory_space=pltpu.VMEM)


def smem():
    return pl.BlockSpec(memory_space=pltpu.SMEM)


def stay(x):
    return pltpu.with_memory_space_constraint(x, pltpu.HBM)


def params():
    return pltpu.CompilerParams(vmem_limit_bytes=VMEM_LIMIT)


def cost(flops, nbytes):
    return pl.CostEstimate(flops=flops, bytes_accessed=nbytes, transcendentals=0)


def f32(*shape):
    return jax.ShapeDtypeStruct(shape, jnp.float32)


def load_kernel(
    density_in, bins_in, colors_in, opacities_in,
    density, bins, depth_even, depth_odd, row_even, row_odd, tables,
    colors, opacities, done,
):
    slices, rows, _ = density.shape
    moves = [
        (density_in, density),
        (bins_in, bins),
        (colors_in, colors),
        (opacities_in, opacities),
    ]
    copies = [pltpu.make_async_copy(a, b, done.at[i]) for i, (a, b) in enumerate(moves)]
    for copy in copies:
        copy.start()
    depth_low = lax.axis_index("depth") & 1 == 0
    tile_low = lax.axis_index("tile") & 1 == 0
    copies[0].wait()
    first, last = density[0], density[slices - 1]
    depth_even[...] = jnp.where(depth_low, last, first)
    depth_odd[...] = jnp.where(depth_low, first, last)
    for k in range(slices):
        top, bottom = density[k, 0:1], density[k, rows - 1 : rows]
        row_even[k : k + 1] = jnp.where(tile_low, bottom, top)
        row_odd[k : k + 1] = jnp.where(tile_low, top, bottom)
    for copy in copies[1:]:
        copy.wait()
    color = whole_number(colors[...], COLOR_ONE)
    opacity = whole_number(opacities[...].reshape(1, -1), OPACITY_ONE)
    words = [color[0:1] | (color[1:2] << 16), color[2:3] | (opacity << 16)]
    for part in range(tables.shape[0]):
        for j in range(2):
            table = words[j][:, part * LANES : (part + 1) * LANES]
            tables[part, j] = jnp.broadcast_to(table, (SUBLANES, LANES))


def trade(x, axis, first):
    slabs, tiles = lax.axis_size("depth"), lax.axis_size("tile")
    pairs = []
    for d in range(slabs):
        for t in range(tiles):
            if axis == "depth":
                inside = 0 <= ((d - first) ^ 1) + first < slabs
                partner = (((d - first) ^ 1) + first, t) if inside else (d, t ^ 1)
            else:
                inside = 0 <= ((t - first) ^ 1) + first < tiles
                partner = (d, ((t - first) ^ 1) + first) if inside else (d ^ 1, t)
            pairs.append((d * tiles + t, partner[0] * tiles + partner[1]))
    return lax.ppermute(x, ("depth", "tile"), pairs)


def whole_number(x, one):
    return (x.astype(jnp.float32) * one).astype(jnp.int32)


def weights_kernel(count, bins, tables, weighted, passed):
    slices, rows, cols = bins.shape
    parts = tables.shape[0]
    table = [[tables[part, j] for j in range(2)] for part in range(parts)]
    occupied = count[0, 0]
    unit = [flag(k < occupied) * (1.0 / OPACITY_ONE) for k in range(slices)]
    for r in range(0, rows, SUBLANES):
        for c in range(0, cols, LANES):
            at = (slice(r, r + SUBLANES), slice(c, c + LANES))
            before = jnp.full((SUBLANES, LANES), 1.0 / COLOR_ONE, jnp.float32)
            for k in range(slices):
                index = bins[(k, *at)]
                lane = index & (LANES - 1)
                found = [lane_lookup(table[0][j], lane) for j in range(2)]
                for part in range(1, parts):
                    later = index >= part * LANES
                    found = [
                        jnp.where(later, lane_lookup(table[part][j], lane), found[j])
                        for j in range(2)
                    ]
                alpha = (found[1] >> 16).astype(jnp.float32) * unit[k]
                weight = before * alpha
                weighted[(0, k, *at)] = weight * (found[0] & 0xFFFF).astype(jnp.float32)
                weighted[(1, k, *at)] = weight * (found[0] >> 16).astype(jnp.float32)
                weighted[(2, k, *at)] = weight * (found[1] & 0xFFFF).astype(jnp.float32)
                before = before - weight
            passed[at] = before * COLOR_ONE


def lane_lookup(table, lane):
    return jnp.take_along_axis(table, lane, axis=1, mode="promise_in_bounds")


def flag(condition):
    return jnp.where(condition, 1.0, 0.0).astype(jnp.float32)


EVEN, ODD = 0, 1


def lower(band):
    tile_is_low = 1 - (lax.axis_index("tile") & 1)
    return tile_is_low if band == EVEN else 1 - tile_is_low


def shade_kernel(stays, bands, density, depth_even, depth_odd, weighted, passed, *rest):
    trades, image = rest[:-1], rest[-1]
    slices, rows, cols = density.shape
    pieces, _, _, piece = image.shape
    me, tile = lax.axis_index("depth"), lax.axis_index("tile")
    bits = [(me >> i) & 1 if stays[i] else 1 - ((me >> i) & 1) for i in range(2)]
    depth_is_low = me & 1 == 0
    has_front, has_behind = flag(me > 0), flag(me < lax.axis_size("depth") - 1)
    inside = flag(jnp.logical_and(tile > 0, tile < lax.axis_size("tile") - 1))
    lane = lax.broadcasted_iota(jnp.int32, (SUBLANES, LANES), 1)
    sub = lax.broadcasted_iota(jnp.int32, (SUBLANES, LANES), 0)
    at_left, at_right = lane == 0, lane == LANES - 1
    at_top, at_bottom = sub == 0, sub == SUBLANES - 1

    for i in range(pieces):
        number = 4 * i + 2 * bits[1] + bits[0]
        for p in range(0, piece, LANES):
            start = pl.multiple_of(number * piece + p, LANES)
            left = pl.multiple_of(jnp.maximum(start - LANES, 0), LANES)
            right = pl.multiple_of(jnp.minimum(start + LANES, cols - LANES), LANES)
            has_left, has_right = flag(start > 0), flag(start + LANES < cols)
            here = pl.ds(start, LANES)
            for n, (band, traded) in enumerate(zip(bands, trades)):
                is_lower = lower(band)
                band_rows = pl.ds(pl.multiple_of(is_lower * SUBLANES, SUBLANES), SUBLANES)
                other_rows = pl.ds(pl.multiple_of((1 - is_lower) * SUBLANES, SUBLANES), SUBLANES)
                is_lower = is_lower == 1
                at = (band_rows, here)
                even_face, odd_face = depth_even[at], depth_odd[at]
                column = [jnp.where(depth_is_low, odd_face, even_face) * has_front]
                column += [density[(k, *at)] for k in range(slices)]
                column += [jnp.where(depth_is_low, even_face, odd_face) * has_behind]
                outside = traded[:, here]
                if band == ODD:
                    outside = outside * inside
                sums = [jnp.zeros((SUBLANES, LANES), jnp.float32) for _ in range(3)]
                for k in range(slices):
                    v = column[k + 1]
                    lv = density[k, band_rows, pl.ds(left, LANES)] * has_left
                    rv = density[k, band_rows, pl.ds(right, LANES)] * has_right
                    plus = jnp.where(at_right, pltpu.roll(rv, LANES - 1, 1), pltpu.roll(v, LANES - 1, 1))
                    minus = jnp.where(at_left, pltpu.roll(lv, 1, 1), pltpu.roll(v, 1, 1))
                    by_col = plus - minus
                    far = jnp.broadcast_to(outside[k : k + 1], (SUBLANES, LANES))
                    other = density[k, other_rows, here]
                    above = jnp.where(is_lower, pltpu.roll(other, 1, 0), far)
                    below = jnp.where(is_lower, far, pltpu.roll(other, SUBLANES - 1, 0))
                    up = jnp.where(at_top, above, pltpu.roll(v, 1, 0))
                    down = jnp.where(at_bottom, below, pltpu.roll(v, SUBLANES - 1, 0))
                    by_row = down - up
                    by_depth = column[k + 2] - column[k]
                    square = by_depth * by_depth + by_row * by_row + by_col * by_col
                    facing = jnp.abs(0.448 * by_depth + 0.42 * by_row + 0.336 * by_col)
                    shade = 0.3 + facing * lax.rsqrt(jnp.maximum(square, 4.0))
                    for channel in range(3):
                        sums[channel] = sums[channel] + weighted[(channel, k, *at)] * shade
                out = (slice(n * SUBLANES, (n + 1) * SUBLANES), slice(p, p + LANES))
                for channel in range(3):
                    image[(i, channel, *out)] = sums[channel]
                image[(i, 3, *out)] = passed[at]


def merged(behind, kept, received):
    front = jnp.where(behind, received, kept)
    back = jnp.where(behind, kept, received)
    light = front[0:3] + front[3:4] * back[0:3]
    return light, front[3] * back[3]


def first_merge_kernel(kept, received, out):
    behind = lax.axis_index("depth") & 1 == 1
    for i in range(kept.shape[0]):
        out[i, 0:3], out[i, 3] = merged(behind, kept[i], received[i])


def merge_kernel(level, bands, kept, *rest):
    me = lax.axis_index("depth")
    behind = (me >> level) & 1 == 1
    bit = (me >> (level + 1)) & 1
    received, (kept_out, *sent) = rest[:bands], rest[bands:]
    height = kept.shape[2] // bands
    for i in range(kept.shape[0] // 2):
        for band in range(bands):
            rows = slice(band * height, (band + 1) * height)
            j = 2 * i + bit
            light, through = merged(behind, kept[j, :, rows], received[band][j])
            kept_out[i, 0:3, rows], kept_out[i, 3, rows] = light, through
            j = 2 * i + 1 - bit
            light, through = merged(behind, kept[j, :, rows], received[band][j])
            sent[band][i, 0:3], sent[band][i, 3] = light, through


def last_merge_kernel(level, bands, kept, *rest):
    behind = (lax.axis_index("depth") >> level) & 1 == 1
    received, out = rest[:bands], rest[bands]
    height = kept.shape[2] // bands
    for band in range(bands):
        rows = slice(band * height, (band + 1) * height)
        light, through = merged(behind, kept[0, :, rows], received[band][0])
        place = pl.ds(pl.multiple_of(lower(band) * SUBLANES, SUBLANES), SUBLANES)
        out[0:3, place], out[3, place] = light, 1.0 - through


def call(kernel, name, out_shape, *args):
    return pl.pallas_call(
        kernel,
        out_shape=out_shape,
        in_specs=[vmem()] * len(args),
        out_specs=jax.tree.map(lambda _: vmem(), out_shape),
        compiler_params=params(),
        name=name,
    )(*args)


def on_device(density, bins, counts, colors, opacities):
    slices, rows, cols = density.shape
    slab_count = lax.axis_size("depth")
    half, piece = slab_count // 2, cols // slab_count
    pixels = rows * cols
    parts = opacities.shape[0] // LANES
    here = pl.BlockSpec(memory_space=pltpu.HBM)
    density, bins, *faces, tables = pl.pallas_call(
        load_kernel,
        out_shape=[
            f32(*density.shape),
            jax.ShapeDtypeStruct(bins.shape, jnp.int32),
            f32(rows, cols),
            f32(rows, cols),
            f32(slices, cols),
            f32(slices, cols),
            jax.ShapeDtypeStruct((parts, 2, SUBLANES, LANES), jnp.int32),
        ],
        in_specs=[here] * 4,
        out_specs=[vmem()] * 7,
        scratch_shapes=[
            pltpu.VMEM(colors.shape, colors.dtype),
            pltpu.VMEM(opacities.shape, opacities.dtype),
            pltpu.SemaphoreType.DMA((4,)),
        ],
        compiler_params=params(),
        name="load",
    )(*(stay(x) for x in (density, bins, colors, opacities)))
    traded = [
        trade(faces[0], "depth", 0),
        trade(faces[1], "depth", 1),
        trade(faces[2], "tile", 0),
        trade(faces[3], "tile", 1),
    ]
    weighted, passed = pl.pallas_call(
        weights_kernel,
        out_shape=[f32(3, slices, rows, cols), f32(rows, cols)],
        in_specs=[smem(), vmem(), vmem()],
        out_specs=[vmem()] * 2,
        compiler_params=params(),
        cost_estimate=cost(64 * slices * pixels, 16 * slices * pixels),
        name="weights",
    )(counts, bins, tables)

    def swap(x, level):
        return lax.ppermute(x, "depth", [(i, i ^ 1 << level) for i in range(slab_count)])

    *faces, row_even, row_odd = traded
    rows_of = {EVEN: row_even, ODD: row_odd}

    def shaded(stays, bands):
        return pl.pallas_call(
            functools.partial(shade_kernel, stays, bands),
            out_shape=f32(half // 2, 4, SUBLANES * len(bands), piece),
            in_specs=[vmem()] * (5 + len(bands)),
            out_specs=vmem(),
            compiler_params=params(),
            cost_estimate=cost(5 * slices * pixels, 2 * slices * pixels),
            name="shade",
        )(density, *faces, weighted, passed, *(rows_of[band] for band in bands))

    levels = slab_count.bit_length() - 1
    bands = (EVEN, ODD)
    sent_far = []
    for band in bands:
        sent = shaded((False, False), (band,))
        received = swap(sent, 0)
        kept = shaded((True, False), (band,))
        _, kept, weighted = lax.optimization_barrier((sent, kept, weighted))
        if sent_far:
            _, kept = lax.optimization_barrier((sent_far[-1], kept))
        sent_far.append(call(first_merge_kernel, "first_merge", f32(*kept.shape), kept, received))
    received = [swap(x, 1) for x in sent_far]
    sent = shaded((False, True), bands)
    received[0], weighted = lax.optimization_barrier((received[0], weighted))
    kept = shaded((True, True), bands)
    kept = call(first_merge_kernel, "first_merge", f32(*kept.shape), kept, swap(sent, 0))
    for level in range(1, levels - 1):
        left = kept.shape[0] // 2
        shapes = [f32(left, 4, rows, piece)] + [f32(left, 4, SUBLANES, piece)] * len(bands)
        kernel = functools.partial(merge_kernel, level, len(bands))
        kept, *sent = call(kernel, "merge", shapes, kept, *received)
        received = [swap(x, level + 1) for x in sent]
    kernel = functools.partial(last_merge_kernel, levels - 1, len(bands))
    return call(kernel, "last_merge", f32(4, rows, piece), kept, *received)


def solution(mesh):
    return jax.shard_map(
        on_device,
        mesh=mesh,
        in_specs=(P("depth", "tile", None), P("depth", "tile", None), P("depth", "tile"), P(), P()),
        out_specs=P(None, "tile", "depth"),
        check_vma=False,
    )
```

```python
import functools

import jax
import jax.numpy as jnp
from jax import lax
from jax.experimental import pallas as pl
from jax.experimental.pallas import tpu as pltpu
from jax.sharding import PartitionSpec as P

LANES = 128
SUBLANES = 8
COLOR_ONE = 4096.0
OPACITY_ONE = 32768.0
VMEM_LIMIT = 12 * 2**20


def vmem():
    return pl.BlockSpec(memory_space=pltpu.VMEM)


def smem():
    return pl.BlockSpec(memory_space=pltpu.SMEM)


def stay(x):
    return pltpu.with_memory_space_constraint(x, pltpu.HBM)


def params():
    return pltpu.CompilerParams(vmem_limit_bytes=VMEM_LIMIT)


def cost(flops, nbytes):
    return pl.CostEstimate(flops=flops, bytes_accessed=nbytes, transcendentals=0)


def f32(*shape):
    return jax.ShapeDtypeStruct(shape, jnp.float32)


def load_kernel(
    density_in, bins_in, colors_in, opacities_in,
    density, bins, depth_even, depth_odd, row_even, row_odd, tables,
    colors, opacities, done,
):
    slices, rows, _ = density.shape
    moves = [
        (density_in, density),
        (bins_in, bins),
        (colors_in, colors),
        (opacities_in, opacities),
    ]
    copies = [pltpu.make_async_copy(a, b, done.at[i]) for i, (a, b) in enumerate(moves)]
    for copy in copies:
        copy.start()
    depth_low = lax.axis_index("depth") & 1 == 0
    tile_low = lax.axis_index("tile") & 1 == 0
    copies[0].wait()
    first, last = density[0], density[slices - 1]
    depth_even[...] = jnp.where(depth_low, last, first)
    depth_odd[...] = jnp.where(depth_low, first, last)
    for k in range(slices):
        top, bottom = density[k, 0:1], density[k, rows - 1 : rows]
        row_even[k : k + 1] = jnp.where(tile_low, bottom, top)
        row_odd[k : k + 1] = jnp.where(tile_low, top, bottom)
    for copy in copies[1:]:
        copy.wait()
    color = whole_number(colors[...], COLOR_ONE)
    opacity = whole_number(opacities[...].reshape(1, -1), OPACITY_ONE)
    words = [color[0:1] | (color[1:2] << 16), color[2:3] | (opacity << 16)]
    for part in range(tables.shape[0]):
        for j in range(2):
            table = words[j][:, part * LANES : (part + 1) * LANES]
            tables[part, j] = jnp.broadcast_to(table, (SUBLANES, LANES))


def trade(x, axis, first):
    slabs, tiles = lax.axis_size("depth"), lax.axis_size("tile")
    pairs = []
    for d in range(slabs):
        for t in range(tiles):
            if axis == "depth":
                inside = 0 <= ((d - first) ^ 1) + first < slabs
                partner = (((d - first) ^ 1) + first, t) if inside else (d, t ^ 1)
            else:
                inside = 0 <= ((t - first) ^ 1) + first < tiles
                partner = (d, ((t - first) ^ 1) + first) if inside else (d ^ 1, t)
            pairs.append((d * tiles + t, partner[0] * tiles + partner[1]))
    return lax.ppermute(x, ("depth", "tile"), pairs)


def whole_number(x, one):
    return (x.astype(jnp.float32) * one).astype(jnp.int32)


def weights_kernel(count, bins, tables, weighted, passed):
    slices, rows, cols = bins.shape
    parts = tables.shape[0]
    table = [[tables[part, j] for j in range(2)] for part in range(parts)]
    occupied = count[0, 0]
    unit = [flag(k < occupied) * (1.0 / OPACITY_ONE) for k in range(slices)]
    for r in range(0, rows, SUBLANES):
        for c in range(0, cols, LANES):
            at = (slice(r, r + SUBLANES), slice(c, c + LANES))
            before = jnp.full((SUBLANES, LANES), 1.0 / COLOR_ONE, jnp.float32)
            for k in range(slices):
                index = bins[(k, *at)]
                lane = index & (LANES - 1)
                found = [lane_lookup(table[0][j], lane) for j in range(2)]
                for part in range(1, parts):
                    later = index >= part * LANES
                    found = [
                        jnp.where(later, lane_lookup(table[part][j], lane), found[j])
                        for j in range(2)
                    ]
                alpha = (found[1] >> 16).astype(jnp.float32) * unit[k]
                weight = before * alpha
                weighted[(0, k, *at)] = weight * (found[0] & 0xFFFF).astype(jnp.float32)
                weighted[(1, k, *at)] = weight * (found[0] >> 16).astype(jnp.float32)
                weighted[(2, k, *at)] = weight * (found[1] & 0xFFFF).astype(jnp.float32)
                before = before - weight
            passed[at] = before * COLOR_ONE


def lane_lookup(table, lane):
    return jnp.take_along_axis(table, lane, axis=1, mode="promise_in_bounds")


def flag(condition):
    return jnp.where(condition, 1.0, 0.0).astype(jnp.float32)


EVEN, ODD = 0, 1


def lower(band):
    tile_is_low = 1 - (lax.axis_index("tile") & 1)
    return tile_is_low if band == EVEN else 1 - tile_is_low


def shade_kernel(stays, bands, density, depth_even, depth_odd, weighted, passed, *rest):
    trades, images = rest[: len(bands)], rest[len(bands) :]
    slices, rows, cols = density.shape
    pieces, _, _, piece = images[0].shape
    planes = 4 * len(bands) // len(images)
    me, tile = lax.axis_index("depth"), lax.axis_index("tile")
    bits = [(me >> i) & 1 if stays[i] else 1 - ((me >> i) & 1) for i in range(2)]
    depth_is_low = me & 1 == 0
    has_front, has_behind = flag(me > 0), flag(me < lax.axis_size("depth") - 1)
    inside = flag(jnp.logical_and(tile > 0, tile < lax.axis_size("tile") - 1))
    lane = lax.broadcasted_iota(jnp.int32, (SUBLANES, LANES), 1)
    sub = lax.broadcasted_iota(jnp.int32, (SUBLANES, LANES), 0)
    at_left, at_right = lane == 0, lane == LANES - 1
    at_top, at_bottom = sub == 0, sub == SUBLANES - 1

    for i in range(pieces):
        number = 4 * i + 2 * bits[1] + bits[0]
        for p in range(0, piece, LANES):
            start = pl.multiple_of(number * piece + p, LANES)
            left = pl.multiple_of(jnp.maximum(start - LANES, 0), LANES)
            right = pl.multiple_of(jnp.minimum(start + LANES, cols - LANES), LANES)
            has_left, has_right = flag(start > 0), flag(start + LANES < cols)
            here = pl.ds(start, LANES)
            for n, (band, traded) in enumerate(zip(bands, trades)):
                is_lower = lower(band)
                band_rows = pl.ds(pl.multiple_of(is_lower * SUBLANES, SUBLANES), SUBLANES)
                other_rows = pl.ds(pl.multiple_of((1 - is_lower) * SUBLANES, SUBLANES), SUBLANES)
                is_lower = is_lower == 1
                at = (band_rows, here)
                even_face, odd_face = depth_even[at], depth_odd[at]
                column = [jnp.where(depth_is_low, odd_face, even_face) * has_front]
                column += [density[(k, *at)] for k in range(slices)]
                column += [jnp.where(depth_is_low, even_face, odd_face) * has_behind]
                outside = traded[:, here]
                if band == ODD:
                    outside = outside * inside
                sums = [jnp.zeros((SUBLANES, LANES), jnp.float32) for _ in range(3)]
                for k in range(slices):
                    v = column[k + 1]
                    lv = density[k, band_rows, pl.ds(left, LANES)] * has_left
                    rv = density[k, band_rows, pl.ds(right, LANES)] * has_right
                    plus = jnp.where(at_right, pltpu.roll(rv, LANES - 1, 1), pltpu.roll(v, LANES - 1, 1))
                    minus = jnp.where(at_left, pltpu.roll(lv, 1, 1), pltpu.roll(v, 1, 1))
                    by_col = plus - minus
                    far = jnp.broadcast_to(outside[k : k + 1], (SUBLANES, LANES))
                    other = density[k, other_rows, here]
                    above = jnp.where(is_lower, pltpu.roll(other, 1, 0), far)
                    below = jnp.where(is_lower, far, pltpu.roll(other, SUBLANES - 1, 0))
                    up = jnp.where(at_top, above, pltpu.roll(v, 1, 0))
                    down = jnp.where(at_bottom, below, pltpu.roll(v, SUBLANES - 1, 0))
                    by_row = down - up
                    by_depth = column[k + 2] - column[k]
                    square = by_depth * by_depth + by_row * by_row + by_col * by_col
                    facing = jnp.abs(0.448 * by_depth + 0.42 * by_row + 0.336 * by_col)
                    shade = 0.3 + facing * lax.rsqrt(jnp.maximum(square, 4.0))
                    for channel in range(3):
                        sums[channel] = sums[channel] + weighted[(channel, k, *at)] * shade
                for channel, value in enumerate([*sums, passed[at]]):
                    image, plane = divmod(4 * n + channel, planes)
                    images[image][i, plane, :, p : p + LANES] = value


def merged(behind, kept, received):
    front = jnp.where(behind, received, kept)
    back = jnp.where(behind, kept, received)
    light = front[0:3] + front[3:4] * back[0:3]
    return light, front[3] * back[3]


def first_merge_kernel(kept, *rest):
    behind = lax.axis_index("depth") & 1 == 1
    received, out = rest[:-1], rest[-1]
    for i in range(kept.shape[0]):
        theirs = jnp.concatenate([x[i] for x in received], 0)
        for at in range(0, kept.shape[1], 4):
            one = slice(at, at + 4)
            out[i, at : at + 3], out[i, at + 3] = merged(behind, kept[i, one], theirs[one])


def merge_kernel(level, bands, kept, *rest):
    me = lax.axis_index("depth")
    behind = (me >> level) & 1 == 1
    bit = (me >> (level + 1)) & 1
    received, (kept_out, *sent) = rest[:bands], rest[bands:]
    for i in range(kept.shape[0] // 2):
        for band in range(bands):
            at = 4 * band
            j = 2 * i + bit
            light, through = merged(behind, kept[j, at : at + 4], received[band][j])
            kept_out[i, at : at + 3], kept_out[i, at + 3] = light, through
            j = 2 * i + 1 - bit
            light, through = merged(behind, kept[j, at : at + 4], received[band][j])
            sent[band][i, 0:3], sent[band][i, 3] = light, through


def last_merge_kernel(level, bands, kept, *rest):
    behind = (lax.axis_index("depth") >> level) & 1 == 1
    received, out = rest[:bands], rest[bands]
    for band in range(bands):
        light, through = merged(behind, kept[0, 4 * band : 4 * band + 4], received[band][0])
        place = pl.ds(pl.multiple_of(lower(band) * SUBLANES, SUBLANES), SUBLANES)
        out[0:3, place], out[3, place] = light, 1.0 - through


def call(kernel, name, out_shape, *args):
    return pl.pallas_call(
        kernel,
        out_shape=out_shape,
        in_specs=[vmem()] * len(args),
        out_specs=jax.tree.map(lambda _: vmem(), out_shape),
        compiler_params=params(),
        name=name,
    )(*args)


def on_device(density, bins, counts, colors, opacities):
    slices, rows, cols = density.shape
    slab_count = lax.axis_size("depth")
    half, piece = slab_count // 2, cols // slab_count
    pixels = rows * cols
    parts = opacities.shape[0] // LANES
    here = pl.BlockSpec(memory_space=pltpu.HBM)
    density, bins, *faces, tables = pl.pallas_call(
        load_kernel,
        out_shape=[
            f32(*density.shape),
            jax.ShapeDtypeStruct(bins.shape, jnp.int32),
            f32(rows, cols),
            f32(rows, cols),
            f32(slices, cols),
            f32(slices, cols),
            jax.ShapeDtypeStruct((parts, 2, SUBLANES, LANES), jnp.int32),
        ],
        in_specs=[here] * 4,
        out_specs=[vmem()] * 7,
        scratch_shapes=[
            pltpu.VMEM(colors.shape, colors.dtype),
            pltpu.VMEM(opacities.shape, opacities.dtype),
            pltpu.SemaphoreType.DMA((4,)),
        ],
        compiler_params=params(),
        name="load",
    )(*(stay(x) for x in (density, bins, colors, opacities)))
    traded = [
        trade(faces[0], "depth", 0),
        trade(faces[1], "depth", 1),
        trade(faces[2], "tile", 0),
        trade(faces[3], "tile", 1),
    ]
    weighted, passed = pl.pallas_call(
        weights_kernel,
        out_shape=[f32(3, slices, rows, cols), f32(rows, cols)],
        in_specs=[smem(), vmem(), vmem()],
        out_specs=[vmem()] * 2,
        compiler_params=params(),
        cost_estimate=cost(64 * slices * pixels, 16 * slices * pixels),
        name="weights",
    )(counts, bins, tables)

    def swap(x, level):
        return lax.ppermute(x, "depth", [(i, i ^ 1 << level) for i in range(slab_count)])

    *faces, row_even, row_odd = traded
    rows_of = {EVEN: row_even, ODD: row_odd}

    def shaded(stays, bands, count=1):
        planes = 4 * len(bands) // count
        return pl.pallas_call(
            functools.partial(shade_kernel, stays, bands),
            out_shape=[f32(half // 2, planes, SUBLANES, piece)] * count,
            in_specs=[vmem()] * (5 + len(bands)),
            out_specs=[vmem()] * count,
            compiler_params=params(),
            cost_estimate=cost(5 * slices * pixels, 2 * slices * pixels),
            name="shade",
        )(density, *faces, weighted, passed, *(rows_of[band] for band in bands))

    levels = slab_count.bit_length() - 1
    bands = (EVEN, ODD)
    sent_far = []
    for band in bands:
        sent = shaded((False, False), (band,), 2 if band == EVEN else 1)
        received = [swap(x, 0) for x in sent]
        (kept,) = shaded((True, False), (band,))
        _, kept, weighted = lax.optimization_barrier((sent, kept, weighted))
        if sent_far:
            _, kept = lax.optimization_barrier((sent_far[-1], kept))
        sent_far.append(call(first_merge_kernel, "first_merge", f32(*kept.shape), kept, *received))
    received = [swap(x, 1) for x in sent_far]
    _, weighted = lax.optimization_barrier((sent_far[-1], weighted))
    near = [swap(x, 0) for x in shaded((False, True), bands, 4)]
    received[0], weighted = lax.optimization_barrier((received[0], weighted))
    (kept,) = shaded((True, True), bands)
    kept = call(first_merge_kernel, "first_merge", f32(*kept.shape), kept, *near)
    for level in range(1, levels - 1):
        left = kept.shape[0] // 2
        shapes = [f32(left, 4 * len(bands), SUBLANES, piece)] + [f32(left, 4, SUBLANES, piece)] * len(bands)
        kernel = functools.partial(merge_kernel, level, len(bands))
        kept, *sent = call(kernel, "merge", shapes, kept, *received)
        received = [swap(x, level + 1) for x in sent]
    kernel = functools.partial(last_merge_kernel, levels - 1, len(bands))
    return call(kernel, "last_merge", f32(4, rows, piece), kept, *received)


def solution(mesh):
    return jax.shard_map(
        on_device,
        mesh=mesh,
        in_specs=(P("depth", "tile", None), P("depth", "tile", None), P("depth", "tile"), P(), P()),
        out_specs=P(None, "tile", "depth"),
        check_vma=False,
    )
```

```python
import functools

import jax
import jax.numpy as jnp
from jax import lax
from jax.experimental import pallas as pl
from jax.experimental.pallas import tpu as pltpu
from jax.sharding import PartitionSpec as P

LANES = 128
SUBLANES = 8
COLOR_ONE = 4096.0
OPACITY_ONE = 32768.0
VMEM_LIMIT = 12 * 2**20


def vmem():
    return pl.BlockSpec(memory_space=pltpu.VMEM)


def smem():
    return pl.BlockSpec(memory_space=pltpu.SMEM)


def stay(x):
    return pltpu.with_memory_space_constraint(x, pltpu.HBM)


def params():
    return pltpu.CompilerParams(vmem_limit_bytes=VMEM_LIMIT)


def cost(flops, nbytes):
    return pl.CostEstimate(flops=flops, bytes_accessed=nbytes, transcendentals=0)


def f32(*shape):
    return jax.ShapeDtypeStruct(shape, jnp.float32)


def load_kernel(
    density_in, bins_in, colors_in, opacities_in,
    density, bins, depth_even, depth_odd, row_even, row_odd, tables,
    colors, opacities, done,
):
    slices, rows, _ = density.shape
    moves = [
        (density_in, density),
        (bins_in, bins),
        (colors_in, colors),
        (opacities_in, opacities),
    ]
    copies = [pltpu.make_async_copy(a, b, done.at[i]) for i, (a, b) in enumerate(moves)]
    for copy in copies:
        copy.start()
    depth_low = lax.axis_index("depth") & 1 == 0
    tile_low = lax.axis_index("tile") & 1 == 0
    copies[0].wait()
    first, last = density[0], density[slices - 1]
    depth_even[...] = jnp.where(depth_low, last, first)
    depth_odd[...] = jnp.where(depth_low, first, last)
    for k in range(slices):
        top, bottom = density[k, 0:1], density[k, rows - 1 : rows]
        row_even[k : k + 1] = jnp.where(tile_low, bottom, top)
        row_odd[k : k + 1] = jnp.where(tile_low, top, bottom)
    for copy in copies[1:]:
        copy.wait()
    color = whole_number(colors[...], COLOR_ONE)
    opacity = whole_number(opacities[...].reshape(1, -1), OPACITY_ONE)
    words = [color[0:1] | (color[1:2] << 16), color[2:3] | (opacity << 16)]
    for part in range(tables.shape[0]):
        for j in range(2):
            table = words[j][:, part * LANES : (part + 1) * LANES]
            tables[part, j] = jnp.broadcast_to(table, (SUBLANES, LANES))


def trade(x, axis, first):
    slabs, tiles = lax.axis_size("depth"), lax.axis_size("tile")
    pairs = []
    for d in range(slabs):
        for t in range(tiles):
            if axis == "depth":
                inside = 0 <= ((d - first) ^ 1) + first < slabs
                partner = (((d - first) ^ 1) + first, t) if inside else (d, t ^ 1)
            else:
                inside = 0 <= ((t - first) ^ 1) + first < tiles
                partner = (d, ((t - first) ^ 1) + first) if inside else (d ^ 1, t)
            pairs.append((d * tiles + t, partner[0] * tiles + partner[1]))
    return lax.ppermute(x, ("depth", "tile"), pairs)


def whole_number(x, one):
    return (x.astype(jnp.float32) * one).astype(jnp.int32)


def weights_kernel(count, bins, tables, weighted, passed):
    slices, rows, cols = bins.shape
    parts = tables.shape[0]
    table = [[tables[part, j] for j in range(2)] for part in range(parts)]
    occupied = count[0, 0]
    unit = [flag(k < occupied) * (1.0 / OPACITY_ONE) for k in range(slices)]
    for r in range(0, rows, SUBLANES):
        for c in range(0, cols, LANES):
            at = (slice(r, r + SUBLANES), slice(c, c + LANES))
            before = jnp.full((SUBLANES, LANES), 1.0 / COLOR_ONE, jnp.float32)
            for k in range(slices):
                index = bins[(k, *at)]
                lane = index & (LANES - 1)
                found = [lane_lookup(table[0][j], lane) for j in range(2)]
                for part in range(1, parts):
                    later = index >= part * LANES
                    found = [
                        jnp.where(later, lane_lookup(table[part][j], lane), found[j])
                        for j in range(2)
                    ]
                alpha = (found[1] >> 16).astype(jnp.float32) * unit[k]
                weight = before * alpha
                weighted[(0, k, *at)] = weight * (found[0] & 0xFFFF).astype(jnp.float32)
                weighted[(1, k, *at)] = weight * (found[0] >> 16).astype(jnp.float32)
                weighted[(2, k, *at)] = weight * (found[1] & 0xFFFF).astype(jnp.float32)
                before = before - weight
            passed[at] = before * COLOR_ONE


def lane_lookup(table, lane):
    return jnp.take_along_axis(table, lane, axis=1, mode="promise_in_bounds")


def flag(condition):
    return jnp.where(condition, 1.0, 0.0).astype(jnp.float32)


EVEN, ODD = 0, 1


def lower(band):
    tile_is_low = 1 - (lax.axis_index("tile") & 1)
    return tile_is_low if band == EVEN else 1 - tile_is_low


def shade_kernel(stays, bands, density, depth_even, depth_odd, weighted, passed, *rest):
    trades, images = rest[: len(bands)], rest[len(bands) :]
    slices, rows, cols = density.shape
    pieces, _, _, piece = images[0].shape
    planes = [(image, i) for image in images for i in range(image.shape[1])]
    me, tile = lax.axis_index("depth"), lax.axis_index("tile")
    bits = [(me >> i) & 1 if stays[i] else 1 - ((me >> i) & 1) for i in range(2)]
    depth_is_low = me & 1 == 0
    has_front, has_behind = flag(me > 0), flag(me < lax.axis_size("depth") - 1)
    inside = flag(jnp.logical_and(tile > 0, tile < lax.axis_size("tile") - 1))
    lane = lax.broadcasted_iota(jnp.int32, (SUBLANES, LANES), 1)
    sub = lax.broadcasted_iota(jnp.int32, (SUBLANES, LANES), 0)
    at_left, at_right = lane == 0, lane == LANES - 1
    at_top, at_bottom = sub == 0, sub == SUBLANES - 1

    for i in range(pieces):
        number = 4 * i + 2 * bits[1] + bits[0]
        for p in range(0, piece, LANES):
            start = pl.multiple_of(number * piece + p, LANES)
            left = pl.multiple_of(jnp.maximum(start - LANES, 0), LANES)
            right = pl.multiple_of(jnp.minimum(start + LANES, cols - LANES), LANES)
            has_left, has_right = flag(start > 0), flag(start + LANES < cols)
            here = pl.ds(start, LANES)
            for n, (band, traded) in enumerate(zip(bands, trades)):
                is_lower = lower(band)
                band_rows = pl.ds(pl.multiple_of(is_lower * SUBLANES, SUBLANES), SUBLANES)
                other_rows = pl.ds(pl.multiple_of((1 - is_lower) * SUBLANES, SUBLANES), SUBLANES)
                is_lower = is_lower == 1
                at = (band_rows, here)
                even_face, odd_face = depth_even[at], depth_odd[at]
                column = [jnp.where(depth_is_low, odd_face, even_face) * has_front]
                column += [density[(k, *at)] for k in range(slices)]
                column += [jnp.where(depth_is_low, even_face, odd_face) * has_behind]
                outside = traded[:, here]
                if band == ODD:
                    outside = outside * inside
                sums = [jnp.zeros((SUBLANES, LANES), jnp.float32) for _ in range(3)]
                for k in range(slices):
                    v = column[k + 1]
                    lv = density[k, band_rows, pl.ds(left, LANES)] * has_left
                    rv = density[k, band_rows, pl.ds(right, LANES)] * has_right
                    plus = jnp.where(at_right, pltpu.roll(rv, LANES - 1, 1), pltpu.roll(v, LANES - 1, 1))
                    minus = jnp.where(at_left, pltpu.roll(lv, 1, 1), pltpu.roll(v, 1, 1))
                    by_col = plus - minus
                    far = jnp.broadcast_to(outside[k : k + 1], (SUBLANES, LANES))
                    other = density[k, other_rows, here]
                    above = jnp.where(is_lower, pltpu.roll(other, 1, 0), far)
                    below = jnp.where(is_lower, far, pltpu.roll(other, SUBLANES - 1, 0))
                    up = jnp.where(at_top, above, pltpu.roll(v, 1, 0))
                    down = jnp.where(at_bottom, below, pltpu.roll(v, SUBLANES - 1, 0))
                    by_row = down - up
                    by_depth = column[k + 2] - column[k]
                    square = by_depth * by_depth + by_row * by_row + by_col * by_col
                    facing = jnp.abs(0.448 * by_depth + 0.42 * by_row + 0.336 * by_col)
                    shade = 0.3 + facing * lax.rsqrt(jnp.maximum(square, 4.0))
                    for channel in range(3):
                        sums[channel] = sums[channel] + weighted[(channel, k, *at)] * shade
                for channel, value in enumerate([*sums, passed[at]]):
                    image, plane = planes[4 * n + channel]
                    image[i, plane, :, p : p + LANES] = value


def merged(behind, kept, received):
    front = jnp.where(behind, received, kept)
    back = jnp.where(behind, kept, received)
    light = front[0:3] + front[3:4] * back[0:3]
    return light, front[3] * back[3]


def first_merge_kernel(kept, *rest):
    behind = lax.axis_index("depth") & 1 == 1
    received, out = rest[:-1], rest[-1]
    for i in range(kept.shape[0]):
        theirs = jnp.concatenate([x[i] for x in received], 0)
        for at in range(0, kept.shape[1], 4):
            one = slice(at, at + 4)
            out[i, at : at + 3], out[i, at + 3] = merged(behind, kept[i, one], theirs[one])


def merge_kernel(level, bands, kept, *rest):
    me = lax.axis_index("depth")
    behind = (me >> level) & 1 == 1
    bit = (me >> (level + 1)) & 1
    received, (kept_out, *sent) = rest[:bands], rest[bands:]
    for i in range(kept.shape[0] // 2):
        for band in range(bands):
            at = 4 * band
            j = 2 * i + bit
            light, through = merged(behind, kept[j, at : at + 4], received[band][j])
            kept_out[i, at : at + 3], kept_out[i, at + 3] = light, through
            j = 2 * i + 1 - bit
            light, through = merged(behind, kept[j, at : at + 4], received[band][j])
            sent[band][i, 0:3], sent[band][i, 3] = light, through


def last_merge_kernel(level, bands, kept, *rest):
    behind = (lax.axis_index("depth") >> level) & 1 == 1
    received, out = rest[:bands], rest[bands]
    for band in range(bands):
        light, through = merged(behind, kept[0, 4 * band : 4 * band + 4], received[band][0])
        place = pl.ds(pl.multiple_of(lower(band) * SUBLANES, SUBLANES), SUBLANES)
        out[0:3, place], out[3, place] = light, 1.0 - through


def call(kernel, name, out_shape, *args):
    return pl.pallas_call(
        kernel,
        out_shape=out_shape,
        in_specs=[vmem()] * len(args),
        out_specs=jax.tree.map(lambda _: vmem(), out_shape),
        compiler_params=params(),
        name=name,
    )(*args)


def on_device(density, bins, counts, colors, opacities):
    slices, rows, cols = density.shape
    slab_count = lax.axis_size("depth")
    half, piece = slab_count // 2, cols // slab_count
    pixels = rows * cols
    parts = opacities.shape[0] // LANES
    here = pl.BlockSpec(memory_space=pltpu.HBM)
    density, bins, *faces, tables = pl.pallas_call(
        load_kernel,
        out_shape=[
            f32(*density.shape),
            jax.ShapeDtypeStruct(bins.shape, jnp.int32),
            f32(rows, cols),
            f32(rows, cols),
            f32(slices, cols),
            f32(slices, cols),
            jax.ShapeDtypeStruct((parts, 2, SUBLANES, LANES), jnp.int32),
        ],
        in_specs=[here] * 4,
        out_specs=[vmem()] * 7,
        scratch_shapes=[
            pltpu.VMEM(colors.shape, colors.dtype),
            pltpu.VMEM(opacities.shape, opacities.dtype),
            pltpu.SemaphoreType.DMA((4,)),
        ],
        compiler_params=params(),
        name="load",
    )(*(stay(x) for x in (density, bins, colors, opacities)))
    traded = [
        trade(faces[0], "depth", 0),
        trade(faces[1], "depth", 1),
        trade(faces[2], "tile", 0),
        trade(faces[3], "tile", 1),
    ]
    weighted, passed = pl.pallas_call(
        weights_kernel,
        out_shape=[f32(3, slices, rows, cols), f32(rows, cols)],
        in_specs=[smem(), vmem(), vmem()],
        out_specs=[vmem()] * 2,
        compiler_params=params(),
        cost_estimate=cost(64 * slices * pixels, 16 * slices * pixels),
        name="weights",
    )(counts, bins, tables)

    def swap(x, level):
        return lax.ppermute(x, "depth", [(i, i ^ 1 << level) for i in range(slab_count)])

    *faces, row_even, row_odd = traded
    rows_of = {EVEN: row_even, ODD: row_odd}

    def shaded(stays, bands, planes):
        return pl.pallas_call(
            functools.partial(shade_kernel, stays, bands),
            out_shape=[f32(half // 2, count, SUBLANES, piece) for count in planes],
            in_specs=[vmem()] * (5 + len(bands)),
            out_specs=[vmem()] * len(planes),
            compiler_params=params(),
            cost_estimate=cost(5 * slices * pixels, 2 * slices * pixels),
            name="shade",
        )(density, *faces, weighted, passed, *(rows_of[band] for band in bands))

    levels = slab_count.bit_length() - 1
    bands = (EVEN, ODD)
    sent_far = []
    for band in bands:
        sent = shaded((False, False), (band,), (4,) if band == EVEN else (4,))
        received = [swap(x, 0) for x in sent]
        (kept,) = shaded((True, False), (band,), (4,))
        _, kept, weighted = lax.optimization_barrier((sent, kept, weighted))
        if sent_far:
            _, kept = lax.optimization_barrier((sent_far[-1], kept))
        sent_far.append(call(first_merge_kernel, "first_merge", f32(*kept.shape), kept, *received))
    received = [swap(x, 1) for x in sent_far]
    _, weighted = lax.optimization_barrier((sent_far[-1], weighted))
    near = [swap(x, 0) for x in shaded((False, True), bands, (3, 3, 2))]
    received[0], weighted = lax.optimization_barrier((received[0], weighted))
    (kept,) = shaded((True, True), bands, (8,))
    kept = call(first_merge_kernel, "first_merge", f32(*kept.shape), kept, *near)
    for level in range(1, levels - 1):
        left = kept.shape[0] // 2
        shapes = [f32(left, 4 * len(bands), SUBLANES, piece)] + [f32(left, 4, SUBLANES, piece)] * len(bands)
        kernel = functools.partial(merge_kernel, level, len(bands))
        kept, *sent = call(kernel, "merge", shapes, kept, *received)
        received = [swap(x, level + 1) for x in sent]
    kernel = functools.partial(last_merge_kernel, levels - 1, len(bands))
    return call(kernel, "last_merge", f32(4, rows, piece), kept, *received)


def solution(mesh):
    return jax.shard_map(
        on_device,
        mesh=mesh,
        in_specs=(P("depth", "tile", None), P("depth", "tile", None), P("depth", "tile"), P(), P()),
        out_specs=P(None, "tile", "depth"),
        check_vma=False,
    )
```

```python
import functools

import jax
import jax.numpy as jnp
from jax import lax
from jax.experimental import pallas as pl
from jax.experimental.pallas import tpu as pltpu
from jax.sharding import PartitionSpec as P

LANES = 128
SUBLANES = 8
COLOR_ONE = 4096.0
OPACITY_ONE = 32768.0
VMEM_LIMIT = 12 * 2**20


def vmem():
    return pl.BlockSpec(memory_space=pltpu.VMEM)


def smem():
    return pl.BlockSpec(memory_space=pltpu.SMEM)


def stay(x):
    return pltpu.with_memory_space_constraint(x, pltpu.HBM)


def params():
    return pltpu.CompilerParams(vmem_limit_bytes=VMEM_LIMIT)


def cost(flops, nbytes):
    return pl.CostEstimate(flops=flops, bytes_accessed=nbytes, transcendentals=0)


def f32(*shape):
    return jax.ShapeDtypeStruct(shape, jnp.float32)


def load_kernel(density_in, density, depth_even, depth_odd, row_even, row_odd, done):
    copy = pltpu.make_async_copy(density_in, density, done)
    copy.start()
    slices, rows, _ = density.shape
    depth_low = lax.axis_index("depth") & 1 == 0
    tile_low = lax.axis_index("tile") & 1 == 0
    copy.wait()
    first, last = density[0], density[slices - 1]
    depth_even[...] = jnp.where(depth_low, last, first)
    depth_odd[...] = jnp.where(depth_low, first, last)
    for k in range(slices):
        top, bottom = density[k, 0:1], density[k, rows - 1 : rows]
        row_even[k : k + 1] = jnp.where(tile_low, bottom, top)
        row_odd[k : k + 1] = jnp.where(tile_low, top, bottom)


def trade(x, axis, first):
    slabs, tiles = lax.axis_size("depth"), lax.axis_size("tile")
    pairs = []
    for d in range(slabs):
        for t in range(tiles):
            if axis == "depth":
                inside = 0 <= ((d - first) ^ 1) + first < slabs
                partner = (((d - first) ^ 1) + first, t) if inside else (d, t ^ 1)
            else:
                inside = 0 <= ((t - first) ^ 1) + first < tiles
                partner = (d, ((t - first) ^ 1) + first) if inside else (d ^ 1, t)
            pairs.append((d * tiles + t, partner[0] * tiles + partner[1]))
    return lax.ppermute(x, ("depth", "tile"), pairs)


def whole_number(x, one):
    return (x.astype(jnp.float32) * one).astype(jnp.int32)


def weights_kernel(
    count, bins_in, colors_in, opacities_in, weighted, passed, bins, colors, opacities, done
):
    moves = [(colors_in, colors), (opacities_in, opacities), (bins_in, bins)]
    copies = [pltpu.make_async_copy(a, b, done.at[i]) for i, (a, b) in enumerate(moves)]
    for copy in copies:
        copy.start()
    slices, rows, cols = bins.shape
    parts = colors.shape[1] // LANES
    copies[0].wait()
    copies[1].wait()
    color = whole_number(colors[...], COLOR_ONE)
    opacity = whole_number(opacities[...].reshape(1, -1), OPACITY_ONE)
    words = [color[0:1] | (color[1:2] << 16), color[2:3] | (opacity << 16)]
    table = [
        [
            jnp.broadcast_to(word[:, part * LANES : (part + 1) * LANES], (SUBLANES, LANES))
            for word in words
        ]
        for part in range(parts)
    ]
    copies[2].wait()
    occupied = count[0, 0]
    unit = [flag(k < occupied) * (1.0 / OPACITY_ONE) for k in range(slices)]
    for r in range(0, rows, SUBLANES):
        for c in range(0, cols, LANES):
            at = (slice(r, r + SUBLANES), slice(c, c + LANES))
            before = jnp.full((SUBLANES, LANES), 1.0 / COLOR_ONE, jnp.float32)
            for k in range(slices):
                index = bins[(k, *at)]
                lane = index & (LANES - 1)
                found = [lane_lookup(table[0][j], lane) for j in range(2)]
                for part in range(1, parts):
                    later = index >= part * LANES
                    found = [
                        jnp.where(later, lane_lookup(table[part][j], lane), found[j])
                        for j in range(2)
                    ]
                alpha = (found[1] >> 16).astype(jnp.float32) * unit[k]
                weight = before * alpha
                weighted[(0, k, *at)] = weight * (found[0] & 0xFFFF).astype(jnp.float32)
                weighted[(1, k, *at)] = weight * (found[0] >> 16).astype(jnp.float32)
                weighted[(2, k, *at)] = weight * (found[1] & 0xFFFF).astype(jnp.float32)
                before = before - weight
            passed[at] = before * COLOR_ONE


def lane_lookup(table, lane):
    return jnp.take_along_axis(table, lane, axis=1, mode="promise_in_bounds")


def flag(condition):
    return jnp.where(condition, 1.0, 0.0).astype(jnp.float32)


EVEN, ODD = 0, 1


def lower(band):
    tile_is_low = 1 - (lax.axis_index("tile") & 1)
    return tile_is_low if band == EVEN else 1 - tile_is_low


def shade_kernel(stays, bands, density, depth_even, depth_odd, weighted, passed, *rest):
    trades, images = rest[: len(bands)], rest[len(bands) :]
    slices, rows, cols = density.shape
    pieces, _, _, piece = images[0].shape
    planes = [(image, i) for image in images for i in range(image.shape[1])]
    me, tile = lax.axis_index("depth"), lax.axis_index("tile")
    bits = [(me >> i) & 1 if stays[i] else 1 - ((me >> i) & 1) for i in range(2)]
    depth_is_low = me & 1 == 0
    has_front, has_behind = flag(me > 0), flag(me < lax.axis_size("depth") - 1)
    inside = flag(jnp.logical_and(tile > 0, tile < lax.axis_size("tile") - 1))
    lane = lax.broadcasted_iota(jnp.int32, (SUBLANES, LANES), 1)
    sub = lax.broadcasted_iota(jnp.int32, (SUBLANES, LANES), 0)
    at_left, at_right = lane == 0, lane == LANES - 1
    at_top, at_bottom = sub == 0, sub == SUBLANES - 1

    for i in range(pieces):
        number = 4 * i + 2 * bits[1] + bits[0]
        for p in range(0, piece, LANES):
            start = pl.multiple_of(number * piece + p, LANES)
            left = pl.multiple_of(jnp.maximum(start - LANES, 0), LANES)
            right = pl.multiple_of(jnp.minimum(start + LANES, cols - LANES), LANES)
            has_left, has_right = flag(start > 0), flag(start + LANES < cols)
            here = pl.ds(start, LANES)
            for n, (band, traded) in enumerate(zip(bands, trades)):
                is_lower = lower(band)
                band_rows = pl.ds(pl.multiple_of(is_lower * SUBLANES, SUBLANES), SUBLANES)
                other_rows = pl.ds(pl.multiple_of((1 - is_lower) * SUBLANES, SUBLANES), SUBLANES)
                is_lower = is_lower == 1
                at = (band_rows, here)
                even_face, odd_face = depth_even[at], depth_odd[at]
                column = [jnp.where(depth_is_low, odd_face, even_face) * has_front]
                column += [density[(k, *at)] for k in range(slices)]
                column += [jnp.where(depth_is_low, even_face, odd_face) * has_behind]
                outside = traded[:, here]
                if band == ODD:
                    outside = outside * inside
                sums = [jnp.zeros((SUBLANES, LANES), jnp.float32) for _ in range(3)]
                for k in range(slices):
                    v = column[k + 1]
                    lv = density[k, band_rows, pl.ds(left, LANES)] * has_left
                    rv = density[k, band_rows, pl.ds(right, LANES)] * has_right
                    plus = jnp.where(at_right, pltpu.roll(rv, LANES - 1, 1), pltpu.roll(v, LANES - 1, 1))
                    minus = jnp.where(at_left, pltpu.roll(lv, 1, 1), pltpu.roll(v, 1, 1))
                    by_col = plus - minus
                    far = jnp.broadcast_to(outside[k : k + 1], (SUBLANES, LANES))
                    other = density[k, other_rows, here]
                    above = jnp.where(is_lower, pltpu.roll(other, 1, 0), far)
                    below = jnp.where(is_lower, far, pltpu.roll(other, SUBLANES - 1, 0))
                    up = jnp.where(at_top, above, pltpu.roll(v, 1, 0))
                    down = jnp.where(at_bottom, below, pltpu.roll(v, SUBLANES - 1, 0))
                    by_row = down - up
                    by_depth = column[k + 2] - column[k]
                    square = by_depth * by_depth + by_row * by_row + by_col * by_col
                    facing = jnp.abs(0.448 * by_depth + 0.42 * by_row + 0.336 * by_col)
                    shade = 0.3 + facing * lax.rsqrt(jnp.maximum(square, 4.0))
                    for channel in range(3):
                        sums[channel] = sums[channel] + weighted[(channel, k, *at)] * shade
                for channel, value in enumerate([*sums, passed[at]]):
                    image, plane = planes[4 * n + channel]
                    image[i, plane, :, p : p + LANES] = value


def merged(behind, kept, received):
    front = jnp.where(behind, received, kept)
    back = jnp.where(behind, kept, received)
    light = front[0:3] + front[3:4] * back[0:3]
    return light, front[3] * back[3]


def first_merge_kernel(kept, *rest):
    behind = lax.axis_index("depth") & 1 == 1
    received, out = rest[:-1], rest[-1]
    for i in range(kept.shape[0]):
        theirs = jnp.concatenate([x[i] for x in received], 0)
        for at in range(0, kept.shape[1], 4):
            one = slice(at, at + 4)
            out[i, at : at + 3], out[i, at + 3] = merged(behind, kept[i, one], theirs[one])


def merge_kernel(level, bands, kept, *rest):
    me = lax.axis_index("depth")
    behind = (me >> level) & 1 == 1
    bit = (me >> (level + 1)) & 1
    received, (kept_out, *sent) = rest[:bands], rest[bands:]
    for i in range(kept.shape[0] // 2):
        for band in range(bands):
            at = 4 * band
            j = 2 * i + bit
            light, through = merged(behind, kept[j, at : at + 4], received[band][j])
            kept_out[i, at : at + 3], kept_out[i, at + 3] = light, through
            j = 2 * i + 1 - bit
            light, through = merged(behind, kept[j, at : at + 4], received[band][j])
            sent[band][i, 0:3], sent[band][i, 3] = light, through


def last_merge_kernel(level, bands, kept, *rest):
    behind = (lax.axis_index("depth") >> level) & 1 == 1
    received, out = rest[:bands], rest[bands]
    for band in range(bands):
        light, through = merged(behind, kept[0, 4 * band : 4 * band + 4], received[band][0])
        place = pl.ds(pl.multiple_of(lower(band) * SUBLANES, SUBLANES), SUBLANES)
        out[0:3, place], out[3, place] = light, 1.0 - through


def call(kernel, name, out_shape, *args):
    return pl.pallas_call(
        kernel,
        out_shape=out_shape,
        in_specs=[vmem()] * len(args),
        out_specs=jax.tree.map(lambda _: vmem(), out_shape),
        compiler_params=params(),
        name=name,
    )(*args)


def on_device(density, bins, counts, colors, opacities):
    slices, rows, cols = density.shape
    slab_count = lax.axis_size("depth")
    half, piece = slab_count // 2, cols // slab_count
    pixels = rows * cols
    here = pl.BlockSpec(memory_space=pltpu.HBM)
    density, *faces = pl.pallas_call(
        load_kernel,
        out_shape=[
            f32(*density.shape),
            f32(rows, cols),
            f32(rows, cols),
            f32(slices, cols),
            f32(slices, cols),
        ],
        in_specs=[here],
        out_specs=[vmem()] * 5,
        scratch_shapes=[pltpu.SemaphoreType.DMA],
        compiler_params=params(),
        name="load",
    )(stay(density))
    traded = [
        trade(faces[0], "depth", 0),
        trade(faces[1], "depth", 1),
        trade(faces[2], "tile", 0),
        trade(faces[3], "tile", 1),
    ]
    weighted, passed = pl.pallas_call(
        weights_kernel,
        out_shape=[f32(3, slices, rows, cols), f32(rows, cols)],
        in_specs=[smem()] + [here] * 3,
        out_specs=[vmem()] * 2,
        scratch_shapes=[
            pltpu.VMEM(bins.shape, jnp.int32),
            pltpu.VMEM(colors.shape, colors.dtype),
            pltpu.VMEM(opacities.shape, opacities.dtype),
            pltpu.SemaphoreType.DMA((3,)),
        ],
        compiler_params=params(),
        cost_estimate=cost(64 * slices * pixels, 16 * slices * pixels),
        name="weights",
    )(counts, stay(bins), stay(colors), stay(opacities))

    def swap(x, level):
        return lax.ppermute(x, "depth", [(i, i ^ 1 << level) for i in range(slab_count)])

    *faces, row_even, row_odd = traded
    rows_of = {EVEN: row_even, ODD: row_odd}

    def shaded(stays, bands, planes):
        return pl.pallas_call(
            functools.partial(shade_kernel, stays, bands),
            out_shape=[f32(half // 2, count, SUBLANES, piece) for count in planes],
            in_specs=[vmem()] * (5 + len(bands)),
            out_specs=[vmem()] * len(planes),
            compiler_params=params(),
            cost_estimate=cost(5 * slices * pixels, 2 * slices * pixels),
            name="shade",
        )(density, *faces, weighted, passed, *(rows_of[band] for band in bands))

    levels = slab_count.bit_length() - 1
    bands = (EVEN, ODD)
    sent_far = []
    for band in bands:
        sent = shaded((False, False), (band,), (4,) if band == EVEN else (4,))
        received = [swap(x, 0) for x in sent]
        (kept,) = shaded((True, False), (band,), (4,))
        _, kept, weighted = lax.optimization_barrier((sent, kept, weighted))
        if sent_far:
            _, kept = lax.optimization_barrier((sent_far[-1], kept))
        sent_far.append(call(first_merge_kernel, "first_merge", f32(*kept.shape), kept, *received))
    received = [swap(x, 1) for x in sent_far]
    _, weighted = lax.optimization_barrier((sent_far[-1], weighted))
    near = [swap(x, 0) for x in shaded((False, True), bands, (3, 3, 2))]
    received[0], weighted = lax.optimization_barrier((received[0], weighted))
    (kept,) = shaded((True, True), bands, (8,))
    kept = call(first_merge_kernel, "first_merge", f32(*kept.shape), kept, *near)
    for level in range(1, levels - 1):
        left = kept.shape[0] // 2
        shapes = [f32(left, 4 * len(bands), SUBLANES, piece)] + [f32(left, 4, SUBLANES, piece)] * len(bands)
        kernel = functools.partial(merge_kernel, level, len(bands))
        kept, *sent = call(kernel, "merge", shapes, kept, *received)
        received = [swap(x, level + 1) for x in sent]
    kernel = functools.partial(last_merge_kernel, levels - 1, len(bands))
    return call(kernel, "last_merge", f32(4, rows, piece), kept, *received)


def solution(mesh):
    return jax.shard_map(
        on_device,
        mesh=mesh,
        in_specs=(P("depth", "tile", None), P("depth", "tile", None), P("depth", "tile"), P(), P()),
        out_specs=P(None, "tile", "depth"),
        check_vma=False,
    )
```

```python
import functools

import jax
import jax.numpy as jnp
from jax import lax
from jax.experimental import pallas as pl
from jax.experimental.pallas import tpu as pltpu
from jax.sharding import PartitionSpec as P

LANES = 128
SUBLANES = 8
COLOR_ONE = 4096.0
OPACITY_ONE = 32768.0
VMEM_LIMIT = 12 * 2**20


def vmem():
    return pl.BlockSpec(memory_space=pltpu.VMEM)


def smem():
    return pl.BlockSpec(memory_space=pltpu.SMEM)


def stay(x):
    return pltpu.with_memory_space_constraint(x, pltpu.HBM)


def params():
    return pltpu.CompilerParams(vmem_limit_bytes=VMEM_LIMIT)


def cost(flops, nbytes):
    return pl.CostEstimate(flops=flops, bytes_accessed=nbytes, transcendentals=0)


def f32(*shape):
    return jax.ShapeDtypeStruct(shape, jnp.float32)


def load_kernel(
    density_in, bins_in, colors_in, opacities_in,
    density, bins, depth_even, depth_odd, row_even, row_odd, tables,
    colors, opacities, done,
):
    slices, rows, _ = density.shape
    moves = [
        (density_in, density),
        (bins_in, bins),
        (colors_in, colors),
        (opacities_in, opacities),
    ]
    copies = [pltpu.make_async_copy(a, b, done.at[i]) for i, (a, b) in enumerate(moves)]
    for copy in copies:
        copy.start()
    depth_low = lax.axis_index("depth") & 1 == 0
    tile_low = lax.axis_index("tile") & 1 == 0
    copies[0].wait()
    first, last = density[0], density[slices - 1]
    depth_even[...] = jnp.where(depth_low, last, first)
    depth_odd[...] = jnp.where(depth_low, first, last)
    for k in range(slices):
        top, bottom = density[k, 0:1], density[k, rows - 1 : rows]
        row_even[k : k + 1] = jnp.where(tile_low, bottom, top)
        row_odd[k : k + 1] = jnp.where(tile_low, top, bottom)
    for copy in copies[1:]:
        copy.wait()
    color = whole_number(colors[...], COLOR_ONE)
    opacity = whole_number(opacities[...].reshape(1, -1), OPACITY_ONE)
    words = [color[0:1] | (color[1:2] << 16), color[2:3] | (opacity << 16)]
    for part in range(tables.shape[0]):
        for j in range(2):
            table = words[j][:, part * LANES : (part + 1) * LANES]
            tables[part, j] = jnp.broadcast_to(table, (SUBLANES, LANES))


def trade(x, axis, first):
    slabs, tiles = lax.axis_size("depth"), lax.axis_size("tile")
    pairs = []
    for d in range(slabs):
        for t in range(tiles):
            if axis == "depth":
                inside = 0 <= ((d - first) ^ 1) + first < slabs
                partner = (((d - first) ^ 1) + first, t) if inside else (d, t ^ 1)
            else:
                inside = 0 <= ((t - first) ^ 1) + first < tiles
                partner = (d, ((t - first) ^ 1) + first) if inside else (d ^ 1, t)
            pairs.append((d * tiles + t, partner[0] * tiles + partner[1]))
    return lax.ppermute(x, ("depth", "tile"), pairs)


def whole_number(x, one):
    return (x.astype(jnp.float32) * one).astype(jnp.int32)


def weights_kernel(count, bins, tables, weighted, passed):
    slices, rows, cols = bins.shape
    parts = tables.shape[0]
    table = [[tables[part, j] for j in range(2)] for part in range(parts)]
    occupied = count[0, 0]
    unit = [flag(k < occupied) * (1.0 / OPACITY_ONE) for k in range(slices)]
    for r in range(0, rows, SUBLANES):
        for c in range(0, cols, LANES):
            at = (slice(r, r + SUBLANES), slice(c, c + LANES))
            before = jnp.full((SUBLANES, LANES), 1.0 / COLOR_ONE, jnp.float32)
            for k in range(slices):
                index = bins[(k, *at)]
                lane = index & (LANES - 1)
                found = [lane_lookup(table[0][j], lane) for j in range(2)]
                for part in range(1, parts):
                    later = index >= part * LANES
                    found = [
                        jnp.where(later, lane_lookup(table[part][j], lane), found[j])
                        for j in range(2)
                    ]
                alpha = (found[1] >> 16).astype(jnp.float32) * unit[k]
                weight = before * alpha
                weighted[(0, k, *at)] = weight * (found[0] & 0xFFFF).astype(jnp.float32)
                weighted[(1, k, *at)] = weight * (found[0] >> 16).astype(jnp.float32)
                weighted[(2, k, *at)] = weight * (found[1] & 0xFFFF).astype(jnp.float32)
                before = before - weight
            passed[at] = before * COLOR_ONE


def lane_lookup(table, lane):
    return jnp.take_along_axis(table, lane, axis=1, mode="promise_in_bounds")


def flag(condition):
    return jnp.where(condition, 1.0, 0.0).astype(jnp.float32)


EVEN, ODD = 0, 1


def lower(band):
    tile_is_low = 1 - (lax.axis_index("tile") & 1)
    return tile_is_low if band == EVEN else 1 - tile_is_low


def shade_kernel(stays, bands, density, depth_odd, depth_even, weighted, passed, *rest):
    trades, images = rest[: len(bands)], rest[len(bands) :]
    slices, rows, cols = density.shape
    pieces, _, _, piece = images[0].shape
    planes = [(image, i) for image in images for i in range(image.shape[1])]
    me, tile = lax.axis_index("depth"), lax.axis_index("tile")
    bits = [(me >> i) & 1 if stays[i] else 1 - ((me >> i) & 1) for i in range(2)]
    depth_is_low = me & 1 == 0
    has_front, has_behind = flag(me > 0), flag(me < lax.axis_size("depth") - 1)
    inside = flag(jnp.logical_and(tile > 0, tile < lax.axis_size("tile") - 1))
    lane = lax.broadcasted_iota(jnp.int32, (SUBLANES, LANES), 1)
    sub = lax.broadcasted_iota(jnp.int32, (SUBLANES, LANES), 0)
    at_left, at_right = lane == 0, lane == LANES - 1
    at_top, at_bottom = sub == 0, sub == SUBLANES - 1

    for i in range(pieces):
        number = 4 * i + 2 * bits[1] + bits[0]
        for p in range(0, piece, LANES):
            start = pl.multiple_of(number * piece + p, LANES)
            left = pl.multiple_of(jnp.maximum(start - LANES, 0), LANES)
            right = pl.multiple_of(jnp.minimum(start + LANES, cols - LANES), LANES)
            has_left, has_right = flag(start > 0), flag(start + LANES < cols)
            here = pl.ds(start, LANES)
            for n, (band, traded) in enumerate(zip(bands, trades)):
                is_lower = lower(band)
                band_rows = pl.ds(pl.multiple_of(is_lower * SUBLANES, SUBLANES), SUBLANES)
                other_rows = pl.ds(pl.multiple_of((1 - is_lower) * SUBLANES, SUBLANES), SUBLANES)
                is_lower = is_lower == 1
                at = (band_rows, here)
                even_face, odd_face = depth_even[at], depth_odd[at]
                column = [jnp.where(depth_is_low, odd_face, even_face) * has_front]
                column += [density[(k, *at)] for k in range(slices)]
                column += [jnp.where(depth_is_low, even_face, odd_face) * has_behind]
                outside = traded[:, here]
                if band == ODD:
                    outside = outside * inside
                sums = [jnp.zeros((SUBLANES, LANES), jnp.float32) for _ in range(3)]
                for k in range(slices):
                    v = column[k + 1]
                    lv = density[k, band_rows, pl.ds(left, LANES)] * has_left
                    rv = density[k, band_rows, pl.ds(right, LANES)] * has_right
                    plus = jnp.where(at_right, pltpu.roll(rv, LANES - 1, 1), pltpu.roll(v, LANES - 1, 1))
                    minus = jnp.where(at_left, pltpu.roll(lv, 1, 1), pltpu.roll(v, 1, 1))
                    by_col = plus - minus
                    far = jnp.broadcast_to(outside[k : k + 1], (SUBLANES, LANES))
                    other = density[k, other_rows, here]
                    above = jnp.where(is_lower, pltpu.roll(other, 1, 0), far)
                    below = jnp.where(is_lower, far, pltpu.roll(other, SUBLANES - 1, 0))
                    up = jnp.where(at_top, above, pltpu.roll(v, 1, 0))
                    down = jnp.where(at_bottom, below, pltpu.roll(v, SUBLANES - 1, 0))
                    by_row = down - up
                    by_depth = column[k + 2] - column[k]
                    square = by_depth * by_depth + by_row * by_row + by_col * by_col
                    facing = jnp.abs(0.448 * by_depth + 0.42 * by_row + 0.336 * by_col)
                    shade = 0.3 + facing * lax.rsqrt(jnp.maximum(square, 4.0))
                    for channel in range(3):
                        sums[channel] = sums[channel] + weighted[(channel, k, *at)] * shade
                for channel, value in enumerate([*sums, passed[at]]):
                    image, plane = planes[4 * n + channel]
                    image[i, plane, :, p : p + LANES] = value


def merged(behind, kept, received):
    front = jnp.where(behind, received, kept)
    back = jnp.where(behind, kept, received)
    light = front[0:3] + front[3:4] * back[0:3]
    return light, front[3] * back[3]


def first_merge_kernel(kept, *rest):
    behind = lax.axis_index("depth") & 1 == 1
    received, out = rest[:-1], rest[-1]
    for i in range(kept.shape[0]):
        theirs = jnp.concatenate([x[i] for x in received], 0)
        for at in range(0, kept.shape[1], 4):
            one = slice(at, at + 4)
            out[i, at : at + 3], out[i, at + 3] = merged(behind, kept[i, one], theirs[one])


def merge_kernel(level, bands, kept, *rest):
    me = lax.axis_index("depth")
    behind = (me >> level) & 1 == 1
    bit = (me >> (level + 1)) & 1
    received, (kept_out, *sent) = rest[:bands], rest[bands:]
    for i in range(kept.shape[0] // 2):
        for band in range(bands):
            at = 4 * band
            j = 2 * i + bit
            light, through = merged(behind, kept[j, at : at + 4], received[band][j])
            kept_out[i, at : at + 3], kept_out[i, at + 3] = light, through
            j = 2 * i + 1 - bit
            light, through = merged(behind, kept[j, at : at + 4], received[band][j])
            sent[band][i, 0:3], sent[band][i, 3] = light, through


def last_merge_kernel(level, bands, kept, *rest):
    behind = (lax.axis_index("depth") >> level) & 1 == 1
    received, out = rest[:bands], rest[bands]
    for band in range(bands):
        light, through = merged(behind, kept[0, 4 * band : 4 * band + 4], received[band][0])
        place = pl.ds(pl.multiple_of(lower(band) * SUBLANES, SUBLANES), SUBLANES)
        out[0:3, place], out[3, place] = light, 1.0 - through


def call(kernel, name, out_shape, *args):
    return pl.pallas_call(
        kernel,
        out_shape=out_shape,
        in_specs=[vmem()] * len(args),
        out_specs=jax.tree.map(lambda _: vmem(), out_shape),
        compiler_params=params(),
        name=name,
    )(*args)


def on_device(density, bins, counts, colors, opacities):
    slices, rows, cols = density.shape
    slab_count = lax.axis_size("depth")
    half, piece = slab_count // 2, cols // slab_count
    pixels = rows * cols
    parts = opacities.shape[0] // LANES
    here = pl.BlockSpec(memory_space=pltpu.HBM)
    density, bins, *faces, tables = pl.pallas_call(
        load_kernel,
        out_shape=[
            f32(*density.shape),
            jax.ShapeDtypeStruct(bins.shape, jnp.int32),
            f32(rows, cols),
            f32(rows, cols),
            f32(slices, cols),
            f32(slices, cols),
            jax.ShapeDtypeStruct((parts, 2, SUBLANES, LANES), jnp.int32),
        ],
        in_specs=[here] * 4,
        out_specs=[vmem()] * 7,
        scratch_shapes=[
            pltpu.VMEM(colors.shape, colors.dtype),
            pltpu.VMEM(opacities.shape, opacities.dtype),
            pltpu.SemaphoreType.DMA((4,)),
        ],
        compiler_params=params(),
        name="load",
    )(*(stay(x) for x in (density, bins, colors, opacities)))
    traded = [
        trade(faces[0], "depth", 0),
        trade(faces[1], "depth", 1),
        trade(faces[2], "tile", 0),
        trade(faces[3], "tile", 1),
    ]
    weighted, passed = pl.pallas_call(
        weights_kernel,
        out_shape=[f32(3, slices, rows, cols), f32(rows, cols)],
        in_specs=[smem(), vmem(), vmem()],
        out_specs=[vmem()] * 2,
        compiler_params=params(),
        cost_estimate=cost(64 * slices * pixels, 16 * slices * pixels),
        name="weights",
    )(counts, bins, tables)

    def swap(x, level):
        return lax.ppermute(x, "depth", [(i, i ^ 1 << level) for i in range(slab_count)])

    *faces, row_even, row_odd = traded
    rows_of = {EVEN: row_even, ODD: row_odd}

    def shaded(stays, bands, planes):
        return pl.pallas_call(
            functools.partial(shade_kernel, stays, bands),
            out_shape=[f32(half // 2, count, SUBLANES, piece) for count in planes],
            in_specs=[vmem()] * (5 + len(bands)),
            out_specs=[vmem()] * len(planes),
            compiler_params=params(),
            cost_estimate=cost(5 * slices * pixels, 2 * slices * pixels),
            name="shade",
        )(density, *faces[::-1], weighted, passed, *(rows_of[band] for band in bands))

    levels = slab_count.bit_length() - 1
    bands = (EVEN, ODD)
    sent_far = []
    for band in bands:
        sent = shaded((False, False), (band,), (4,) if band == EVEN else (4,))
        received = [swap(x, 0) for x in sent]
        (kept,) = shaded((True, False), (band,), (4,))
        _, kept, weighted = lax.optimization_barrier((sent, kept, weighted))
        if sent_far:
            _, kept = lax.optimization_barrier((sent_far[-1], kept))
        sent_far.append(call(first_merge_kernel, "first_merge", f32(*kept.shape), kept, *received))
    received = [swap(x, 1) for x in sent_far]
    _, weighted = lax.optimization_barrier((sent_far[-1], weighted))
    near = [swap(x, 0) for x in shaded((False, True), bands, (3, 3, 2))]
    received[0], weighted = lax.optimization_barrier((received[0], weighted))
    (kept,) = shaded((True, True), bands, (8,))
    kept = call(first_merge_kernel, "first_merge", f32(*kept.shape), kept, *near)
    for level in range(1, levels - 1):
        left = kept.shape[0] // 2
        shapes = [f32(left, 4 * len(bands), SUBLANES, piece)] + [f32(left, 4, SUBLANES, piece)] * len(bands)
        kernel = functools.partial(merge_kernel, level, len(bands))
        kept, *sent = call(kernel, "merge", shapes, kept, *received)
        received = [swap(x, level + 1) for x in sent]
    kernel = functools.partial(last_merge_kernel, levels - 1, len(bands))
    return call(kernel, "last_merge", f32(4, rows, piece), kept, *received)


def solution(mesh):
    return jax.shard_map(
        on_device,
        mesh=mesh,
        in_specs=(P("depth", "tile", None), P("depth", "tile", None), P("depth", "tile"), P(), P()),
        out_specs=P(None, "tile", "depth"),
        check_vma=False,
    )
```
